128 devices in a mesh: stream: 16 (over y, x), span: 8 (over z, core).
Axes of the slice: x: 4, y: 4, z: 4, core: 2. Of those that a mesh axis runs over, the one named last changes fastest.
Arguments:
- fluid_pos: float32 [128, 64, 3, 128], P('stream', 'span'), may hold values from 0 to 1
- fluid_vel: float32 [128, 64, 3, 128], P('stream', 'span'), may hold values from -6 to 6
- fluid_mass: float32 [128, 64, 128], P('stream', 'span'), may hold values from 0.5 to 2
- fluid_count: int32 [128, 64], P('stream', 'span'), may hold values from 64 to 128
- clump_center: float32 [65536, 3], P(('stream', 'span')), may hold values from 0 to 1
- clump_vel: float32 [65536, 3], P(('stream', 'span')), may hold values from -6 to 6
- clump_arm: float32 [65536, 3, 128], P(('stream', 'span')), may hold values from -1.8 to 1.8
- margin_device: int32 [65536, 2], P(('stream', 'span')), may hold values from 0 to 127, all different within a row; in each aligned block of 512 rows (0 to 511, 512 to 1023, ...) at most 16 rows name the same one
- margin_block: int32 [65536, 2], P(('stream', 'span')), may hold values from 0 to 63
- margin_offset: float32 [65536, 2, 3], P(('stream', 'span')), may hold values from 0 to 1
- contact_partner: int32 [65536], P(('stream', 'span')), may hold values from 0 to 1023
Outputs:
- fluid_density: float32 [128, 64, 128], P('stream', 'span')
- clump_load: float32 [6, 65536], P(None, ('stream', 'span'))
The draws below stay inside these ranges and needn't reach their ends.
Inputs may be any that keep to these rules, and one draw needn't show every extreme that they name: `margin_device`: among the 1024 margins of one device's clumps, at most 16 name any one device, and some device is named exactly 16 times; the two margins of a clump name different devices.
All inputs are finite; a program needn't handle non-finite values.
Results may differ from the reference program's by a relative error of at most 0.0001.
Values sent between devices are 32-bit elements; how exact they have to be, the bound alone decides.
No kernel may reach another device: no remote copies, remote signals or barrier semaphores. Data moves between devices by JAX's collectives and lax.ppermute only.
A program may use at most 128 MiB of HBM per device.

```python
import math
import jax
import jax.numpy as jnp
import numpy as np
from jax import lax

FBX = 8
FBY = 8
PB = 128
SPH = 128
CL = 512
CAP = 16
NXB = 128
NYB = 64
CLUMPS = 65536
N_SPAN = 8
DEVICES = 128


def with_ends(entries, key, least, largest):
    spot = [jax.random.randint(jax.random.fold_in(key, axis), (), 0, length) for axis, length in enumerate(entries.shape)]
    main_axis = entries.shape.index(max(entries.shape))
    next_to = spot[:main_axis] + [(spot[main_axis] + 1) % entries.shape[main_axis]] + spot[main_axis + 1:]
    return entries.at[tuple(spot)].set(least).at[tuple(next_to)].set(largest)


def block_scale(own_key, shape, cuts, low, high):
    level, own = 1.0, jax.random.fold_in(own_key, 6)
    for position, blocks in cuts:
        heights = jnp.exp(jax.random.uniform(jax.random.fold_in(own, position), (blocks,), jnp.float32, low / len(cuts), high / len(cuts)))
        level = level * jnp.repeat(heights, shape[position] // blocks).reshape([-1 if axis == position else 1 for axis in range(len(shape))])
    return level


def deal_out(rng, own, number, rows, amount, top, limit, slope):
    sequence = jax.random.permutation(rng, amount)
    crowded, usual = load_shares(amount, rows * top, limit, slope, True), load_shares(amount, rows * top, limit, slope, False)
    places = jnp.arange(amount)

    def named(lengths, turn):
        used = int((lengths > 0).sum())
        fixed = max(1, used // 4)
        passed = fixed + (places - fixed + turn * (used - fixed)) % max(1, amount - fixed)
        return jnp.zeros((amount,), jnp.int32).at[sequence[jnp.where(places < fixed, places, passed)]].set(jnp.asarray(lengths, jnp.int32))

    lengths = jnp.where(number % 4 == 0, named(crowded, number // 4), named(usual, number - number // 4 - 1))
    mixed = jax.random.permutation(jax.random.fold_in(own, 3), amount)
    source_of, receiver = mixed[0:amount // 2 * 2:2], mixed[1:amount // 2 * 2:2]
    margin = jnp.minimum(lengths[source_of] - 1, limit - lengths[receiver]) // 2
    margin = jnp.where((source_of == sequence[0]) | (receiver == sequence[0]) | (lengths[receiver] == 0), 0, jnp.maximum(margin, 0))
    passed = jax.random.randint(jax.random.fold_in(own, 4), (amount // 2,), 0, 1 << 20) % (margin + 1)
    lengths = lengths.at[source_of].add(-passed).at[receiver].add(passed)
    members = jnp.searchsorted(jnp.cumsum(lengths), jnp.arange(rows * top), side="right").astype(jnp.int32)
    listing = members.reshape(top, rows).T
    listing = listing[jax.random.permutation(jax.random.fold_in(own, 1), rows)]
    turn = jax.random.randint(jax.random.fold_in(own, 2), (rows, 1), 0, top)
    return jnp.take_along_axis(listing, (jnp.arange(top)[None, :] + turn) % top, axis=1)


def load_shares(count, total, limit, slope, full):
    weights = [(1 << 20) // math.isqrt(rank ** slope) + 1 for rank in range(1, count + 1)]
    largest = limit if full else min(limit, max(-(-total // count), total * weights[0] // sum(weights)))
    least = 1 if total - largest >= count - 1 else 0
    counts, spare = [largest] + [least] * (count - 1), total - largest - least * (count - 1)
    while spare > 0:
        free = [i for i in range(1, count) if counts[i] < largest] or [i for i in range(1, count) if counts[i] < limit]
        mass, budget = sum([weights[i] for i in free]), spare
        for i in free:
            extra = min(limit - counts[i], max(1, budget * weights[i] // mass), spare)
            counts[i] = counts[i] + extra
            spare = spare - extra
    return np.array(counts)


def bell_draw(own_key, shape, spread, most, cuts=(), held_as=jnp.bfloat16):
    gain = block_scale(own_key, shape, cuts, -0.22, 0.18) if cuts else 1.0
    values = jax.random.normal(own_key, shape, jnp.float32) * spread * gain
    return jnp.minimum(jnp.maximum(values, -most), most).astype(held_as)


def setup_inputs(seed: int = 0) -> dict:
    seeds = jax.random.split(jax.random.key(seed), 12)
    fluid_pos = jnp.clip(1.0 * jax.random.uniform(seeds[0], (NXB, NYB, 3, PB), jnp.float32) ** block_scale(seeds[0], (NXB, NYB, 3, PB), ((0, 16), (1, 8)), -0.2, 0.2), 0.0, 1.0)
    fluid_vel = bell_draw(seeds[1], (NXB, NYB, 3, PB), 1.0, 6.0, ((0, 16), (1, 8)), jnp.float32)
    fluid_mass = jnp.clip(jnp.exp(math.log(2.0) - 1.3862944 * jax.random.uniform(seeds[2], (NXB, NYB, PB), jnp.float32) ** block_scale(seeds[2], (NXB, NYB, PB), ((0, 16), (1, 8)), -0.2, 0.2)), 0.5, 2.0)
    fluid_count = with_ends(jax.random.randint(seeds[3], (NXB, NYB), PB // 2, PB + 1), jax.random.fold_in(seeds[3], 1), PB // 2, PB).astype(jnp.int32)
    clump_center = jnp.clip(1.0 * jax.random.uniform(seeds[4], (CLUMPS, 3), jnp.float32) ** block_scale(seeds[4], (CLUMPS, 3), ((0, 128),), -0.2, 0.2), 0.0, 1.0)
    clump_vel = bell_draw(seeds[5], (CLUMPS, 3), 1.0, 6.0, ((0, 128),), jnp.float32)
    clump_arm = bell_draw(seeds[6], (CLUMPS, 3, SPH), 0.3, 1.8, ((0, 128),), jnp.float32)
    margin_device_keys = jax.random.split(jax.random.fold_in(seeds[7], 1), CLUMPS // CL)
    margin_device_turns = jax.random.permutation(jax.random.fold_in(seeds[7], 3), CLUMPS // CL)
    margin_device = jax.vmap(lambda own, number: deal_out(jax.random.fold_in(seeds[7], 2), own, number, CL, DEVICES, 2, CAP, 2))(margin_device_keys, margin_device_turns).reshape((CLUMPS, 2))
    margin_block = with_ends(jax.random.randint(seeds[8], (CLUMPS, 2), 0, FBX * FBY), jax.random.fold_in(seeds[8], 1), 0, (FBX * FBY) - 1).astype(jnp.int32)
    margin_offset = jnp.clip(1.0 * jax.random.uniform(seeds[9], (CLUMPS, 2, 3), jnp.float32) ** block_scale(seeds[9], (CLUMPS, 2, 3), ((0, 128),), -0.2, 0.2), 0.0, 1.0)
    contact_partner = with_ends(jax.random.randint(seeds[10], (CLUMPS,), 0, 2 * CL), jax.random.fold_in(seeds[10], 1), 0, (2 * CL) - 1).astype(jnp.int32)
    return dict(fluid_pos=fluid_pos, fluid_vel=fluid_vel, fluid_mass=fluid_mass, fluid_count=fluid_count, clump_center=clump_center, clump_vel=clump_vel, clump_arm=clump_arm, margin_device=margin_device, margin_block=margin_block, margin_offset=margin_offset, contact_partner=contact_partner)


H_SQ = 0.25
SIG_SQ = 0.5
DENS = 0.03125
DRAG = 0.002
STIFF = 0.005


def particle_mask(fluid_count, width):
    lanes = jnp.arange(width, dtype=jnp.int32)
    return (lanes[None, None, :] < fluid_count[..., None]).astype(jnp.float32)


def pair_sum(center, neigh, shift_x, shift_y):
    delta_x = center[:, 0, :, None] - neigh[:, 0, None, :] - shift_x
    delta_y = center[:, 1, :, None] - neigh[:, 1, None, :] - shift_y
    delta_z = center[:, 2, :, None] - neigh[:, 2, None, :]
    kernel = jnp.exp(-(delta_x * delta_x + delta_y * delta_y + delta_z * delta_z) / H_SQ)
    return jnp.sum(kernel * neigh[:, 3, None, :], axis=2)


def tile_force(pos, amp, offset, arm, velocity):
    spot = offset[:, None] + arm
    delta = pos[:, :, None] - spot[:, None, :]
    kernel = jnp.exp(-jnp.sum(delta * delta, axis=0) / H_SQ)
    acc = jnp.dot(amp, kernel, precision=lax.Precision.HIGHEST)
    return DRAG * (acc[:3] - velocity[:, None] * acc[3][None, :])


def contact_force(mine, other):
    delta = mine[:, :, None] - other[:, None, :]
    kernel = jnp.exp(-jnp.sum(delta * delta, axis=0) / SIG_SQ)
    pulled = jnp.dot(other, kernel.T, precision=lax.Precision.HIGHEST)
    return STIFF * (mine * jnp.sum(kernel, axis=1)[None, :] - pulled)


def reference(fluid_pos, fluid_vel, fluid_mass, fluid_count, clump_center, clump_vel, clump_arm, margin_device, margin_block, margin_offset, contact_partner):
    rows_x, rows_y, width = fluid_mass.shape
    live = particle_mask(fluid_count, width)
    packed = jnp.concatenate([fluid_pos, (live * fluid_mass)[:, :, None, :]], axis=2)
    padded = jnp.pad(packed, ((1, 1), (1, 1), (0, 0), (0, 0)))

    def one_row(row):
        center = lax.dynamic_index_in_dim(padded, row + 1, 0, keepdims=False)[1:-1]
        total = jnp.zeros((rows_y, width), jnp.float32)
        for step_x in (-1, 0, 1):
            line = lax.dynamic_index_in_dim(padded, row + 1 + step_x, 0, keepdims=False)
            for step_y in (-1, 0, 1):
                total = total + pair_sum(center, line[1 + step_y:1 + step_y + rows_y], float(step_x), float(step_y))
        return total

    sums = lax.map(one_row, jnp.arange(rows_x, dtype=jnp.int32))
    fluid_density = DENS * (fluid_mass + sums)
    weight = live * fluid_mass / fluid_density
    amp = jnp.concatenate([fluid_vel * weight[:, :, None, :], weight[:, :, None, :]], axis=2)
    pos_table = fluid_pos.reshape(rows_x * rows_y, 3, width)
    amp_table = amp.reshape(rows_x * rows_y, 4, width)
    global_x = (margin_device // N_SPAN) * FBX + margin_block // FBY
    global_y = (margin_device % N_SPAN) * FBY + margin_block % FBY
    flat_block = (global_x * rows_y + global_y).astype(jnp.int32)
    owner = jnp.arange(CLUMPS, dtype=jnp.int32) // CL
    partner = ((owner * CL + contact_partner) % CLUMPS).astype(jnp.int32)
    world = clump_center[:, :, None] + clump_arm

    def one_clump(item):
        blocks, offsets, arm, velocity, mine, partner_index = item
        force = tile_force(pos_table[blocks[0]], amp_table[blocks[0]], offsets[0], arm, velocity)
        force = force + tile_force(pos_table[blocks[1]], amp_table[blocks[1]], offsets[1], arm, velocity)
        force = force + contact_force(mine, world[partner_index])
        torque = jnp.cross(arm, force, axis=0)
        return jnp.concatenate([jnp.sum(force, axis=1), jnp.sum(torque, axis=1)])

    loads = lax.map(one_clump, (flat_block, margin_offset, clump_arm, clump_vel, world, partner), batch_size=64)
    return fluid_density, loads.T
```

```python
import functools
import math

import jax
import jax.numpy as jnp
from jax import lax
from jax.experimental import pallas as pl
from jax.experimental.pallas import tpu as pltpu
from jax.sharding import PartitionSpec as P

H_SQ = 0.25
SIG_SQ = 0.5
DENS = 0.03125
DRAG = 0.002
STIFF = 0.005
LOG2E = math.log2(math.e)
C_FLUID = LOG2E / H_SQ
C_CONTACT = LOG2E / SIG_SQ
AXES = ("stream", "span")
W = 128
FEATS = 32
DEAD = -30000.0
BF = jnp.bfloat16
F32 = jnp.float32


def split3(v):
    hi = v.astype(BF).astype(F32)
    rest = v - hi
    mid = rest.astype(BF).astype(F32)
    return hi, mid, rest - mid


def norm_of(x, y, z, coef):
    return (x * x + y * y + z * z) * (-coef)


def left_rows(xs, ys, zs, norm):
    h, m, low = ([c[i] for c in (xs, ys, zs)] for i in range(3))
    one = jnp.ones_like(h[0])
    return h + h + h + m + m + low + list(split3(norm)) + [one, one, one]


def right_rows(xs, ys, zs, norm):
    h, m, low = ([c[i] for c in (xs, ys, zs)] for i in range(3))
    one = jnp.ones_like(h[0])
    return h + m + low + h + m + h + [one, one, one] + list(split3(norm))


def put_rows(ref, rows, base=0):
    for i, row in enumerate(rows):
        ref[base + 8 * i : base + 8 * i + 8, :] = row


def zero_tail(ref, base=0):
    zero = jnp.zeros((8, W), F32)
    for i in range(24, FEATS):
        ref[base + 8 * i : base + 8 * i + 8, :] = zero


def take_rows(ref, j, base=0):
    return ref[pl.ds(base + j, FEATS, stride=8), :]


def gauss(left, right):
    return jnp.exp2(jnp.dot(left, right, preferred_element_type=F32))


def two_halves(kernel):
    hi = kernel.astype(BF)
    lo = (kernel - hi.astype(F32)).astype(BF)
    return jnp.concatenate([hi, lo], axis=0)


def lane_sum(v):
    return jnp.sum(v, axis=1, keepdims=True)


def prep_kernel(dev_ref, blk_ref, dev_s, off_s, arm_ref, first_ref, second_ref, ids_ref, rank_ref,
                buf, rank_s, sems):
    entries = dev_ref.shape[1]
    parts = entries // W
    dev = dev_ref[...]
    row = lax.broadcasted_iota(jnp.int32, (W, entries), 0)
    hot = (row == dev).astype(F32)
    hot_b = hot.astype(BF)
    up = lax.broadcasted_iota(jnp.int32, (W, 2 * W), 0)
    lane = lax.broadcasted_iota(jnp.int32, (W, 2 * W), 1)
    tri = jnp.where(lane >= W, 1.0, jnp.where(up < lane, 1.0, 0.0)).astype(BF)
    carry = jnp.zeros((W, W), F32)
    ranks = []
    for part in range(parts):
        piece = slice(part * W, part * W + W)
        both = jnp.dot(hot_b[:, piece], tri, preferred_element_type=F32)
        ranks.append(jnp.sum(hot[:, piece] * (both[:, :W] + carry), axis=0, keepdims=True))
        carry = carry + both[:, W:]
    rank = jnp.concatenate(ranks, axis=1).astype(jnp.int32)
    rank_ref[...] = rank
    move = pltpu.make_async_copy(rank_ref, rank_s, sems.at[0])
    move.start()
    named = jnp.where(row == rank, blk_ref[...] + 1, 0).astype(F32).astype(BF)
    ids = lax.dot_general(hot_b, named, (((1,), (1,)), ((), ())), preferred_element_type=F32)
    ids_ref[...] = ids.astype(jnp.int32) - 1
    move.wait()

    clumps = entries // 2

    def step(i, carry):
        for k in range(2):
            for j in range(8):
                c = i * 8 + j
                e = k * clumps + c
                d = dev_s[0, e]
                r = rank_s[0, e]
                base = ((r >> 3) * W + d) * 24 + (r & 7)
                for q in range(3):
                    buf[pl.ds(base + 8 * q, 1), :] = (
                        arm_ref[q, pl.ds(c, 1), :] + off_s[q, e]
                    )
        return carry

    lax.fori_loop(0, clumps // 8, step, 0)
    half = W * 24
    one = pltpu.make_async_copy(buf.at[pl.ds(0, half)], first_ref, sems.at[0])
    two = pltpu.make_async_copy(buf.at[pl.ds(half, half)], second_ref, sems.at[1])
    one.start()
    two.start()
    one.wait()
    two.wait()


def prep(dev, blk, off, arms):
    entries = dev.shape[1]
    vm = pl.BlockSpec(memory_space=pltpu.VMEM)
    sm = pl.BlockSpec(memory_space=pltpu.SMEM)
    hbm = pl.BlockSpec(memory_space=pl.ANY)
    send = jax.ShapeDtypeStruct((W * 24, W), F32)
    return pl.pallas_call(
        prep_kernel,
        out_shape=(
            send,
            send,
            jax.ShapeDtypeStruct((W, W), jnp.int32),
            jax.ShapeDtypeStruct((1, entries), jnp.int32),
        ),
        in_specs=[vm, vm, sm, sm, vm],
        out_specs=(hbm, hbm, vm, vm),
        scratch_shapes=[
            pltpu.VMEM((2 * W * 24, W), F32),
            pltpu.SMEM((1, entries), jnp.int32),
            pltpu.SemaphoreType.DMA((2,)),
        ],
        compiler_params=pltpu.CompilerParams(vmem_limit_bytes=24 << 20),
        name="prep",
    )(dev, blk, dev, off, arms)


def density_kernel(ext_ref, own_ref, mass_ref, vel_ref, dens_ref, table_ref, amp_ref,
                   feat, right, sums, left, wide):
    rows_y = 8
    zero_tail(feat)
    for s in range(9):
        zero_tail(right, s * FEATS * 8)

    def coords(ref, at):
        return [ref[q, pl.ds(at, 8), :] - 0.5 for q in range(3)]

    def ext_group(g, carry):
        at = pl.multiple_of(g * 8, 8)
        x, y, z = coords(ext_ref, at)
        m = ext_ref[3, pl.ds(at, 8), :]
        logm = jnp.where(m > 0.0, jnp.log2(jnp.where(m > 0.0, m, 1.0)), DEAD)
        norm = norm_of(x, y, z, C_FLUID) + logm
        put_rows(feat, left_rows(split3(x), split3(y), split3(z), norm))
        for j in range(8):
            left[at + j] = jnp.transpose(take_rows(feat, j)).astype(BF)
        return carry

    lax.fori_loop(0, ext_ref.shape[1] // 8, ext_group, 0)

    def own_row(a, carry):
        at = pl.multiple_of(a * 8, 8)
        x, y, z = coords(own_ref, at)
        xs = [x + 1.0, x, x - 1.0]
        ys = [y + 1.0, y, y - 1.0]
        scale = 2.0 * C_FLUID
        xsplit = [split3(v * scale) for v in xs]
        ysplit = [split3(v * scale) for v in ys]
        zsplit = split3(z * scale)
        for ix in range(3):
            for iy in range(3):
                norm = norm_of(xs[ix], ys[iy], z, C_FLUID)
                put_rows(right, right_rows(xsplit[ix], ysplit[iy], zsplit, norm),
                         (ix * 3 + iy) * FEATS * 8)

        def block(b, inner):
            total = jnp.zeros((8, W), F32)
            for ix in range(3):
                for iy in range(3):
                    rhs = take_rows(right, b, (ix * 3 + iy) * FEATS * 8).astype(BF)
                    lhs = left[(a + ix) * 10 + b + iy]
                    total = total + jnp.sum(gauss(lhs, rhs).reshape(16, 8, W), axis=0)
            sums[pl.ds(b, 1), :] = jnp.sum(total, axis=0, keepdims=True)
            return inner

        lax.fori_loop(0, rows_y, block, 0)
        density = DENS * (mass_ref[pl.ds(at, 8), :] + sums[...])
        dens_ref[pl.ds(at, 8), :] = density
        weight = own_ref[3, pl.ds(at, 8), :] / density
        parts = [vel_ref[q, pl.ds(at, 8), :] * weight for q in range(3)] + [weight]
        zero = jnp.zeros((8, W), F32)
        for q, v in enumerate(parts):
            hi = v.astype(BF).astype(F32)
            wide[8 * q : 8 * q + 8, :] = hi
            wide[8 * (q + 8) : 8 * (q + 8) + 8, :] = v - hi
        for q in (4, 5, 6, 7, 12, 13, 14, 15):
            wide[8 * q : 8 * q + 8, :] = zero
        norm = norm_of(x, y, z, C_FLUID)
        put_rows(feat, left_rows(split3(x), split3(y), split3(z), norm))
        upper = lax.broadcasted_iota(jnp.int32, (16, W), 0) < 8
        for j in range(8):
            table_ref[at + j] = jnp.transpose(take_rows(feat, j)).astype(BF)
            a16 = wide[pl.ds(j, 16, stride=8), :]
            amp_ref[at + j, :, 0:W] = a16.astype(BF)
            amp_ref[at + j, :, W : 2 * W] = jnp.where(upper, a16, 0.0).astype(BF)
        return carry

    lax.fori_loop(0, 8, own_row, 0)


def density(ext, own, mass, vel):
    blocks = mass.shape[0]
    vm = pl.BlockSpec(memory_space=pltpu.VMEM)
    return pl.pallas_call(
        density_kernel,
        out_shape=(
            jax.ShapeDtypeStruct((blocks, W), F32),
            jax.ShapeDtypeStruct((blocks, W, FEATS), BF),
            jax.ShapeDtypeStruct((blocks, 16, 2 * W), BF),
        ),
        in_specs=[vm] * 4,
        out_specs=(vm, vm, vm),
        scratch_shapes=[
            pltpu.VMEM((FEATS * 8, W), F32),
            pltpu.VMEM((9 * FEATS * 8, W), F32),
            pltpu.VMEM((8, W), F32),
            pltpu.VMEM((ext.shape[1], W, FEATS), BF),
            pltpu.VMEM((W, W), F32),
        ],
        compiler_params=pltpu.CompilerParams(vmem_limit_bytes=24 << 20),
        name="density",
    )(ext, own, mass, vel)


def columns_to_lanes(cols):
    lane = lax.broadcasted_iota(jnp.int32, (8, W), 1)
    out = jnp.zeros((8, W), F32)
    for q, col in enumerate(cols):
        out = jnp.where(lane == q, col, out)
    return out


def contact_kernel(partner_s, arm_ref, world_ref, next_ref, out_ref, cand, gat, feat, right, lead, acc):
    clumps = arm_ref.shape[1]
    cand[:, 0:clumps, :] = world_ref[...]
    cand[:, clumps : 2 * clumps, :] = next_ref[...]
    zero_tail(feat)
    zero_tail(right)
    zero = jnp.zeros((8, W), F32)
    for q in (4, 5, 6, 7, 12, 13, 14, 15):
        lead[8 * q : 8 * q + 8, :] = zero
    upper = lax.broadcasted_iota(jnp.int32, (16, W), 0) < 8

    def group(g, carry):
        at = pl.multiple_of(g * 8, 8)
        for j in range(8):
            p = partner_s[0, at + j]
            for q in range(3):
                gat[8 * q + j : 8 * q + j + 1, :] = cand[q, pl.ds(p, 1), :]
        zb = [gat[8 * q : 8 * q + 8, :] - 0.5 for q in range(3)]
        za = [world_ref[q, pl.ds(at, 8), :] - 0.5 for q in range(3)]
        put_rows(feat, left_rows(*[split3(v) for v in zb], norm_of(*zb, C_CONTACT)))
        scaled = [split3(v * (2.0 * C_CONTACT)) for v in za]
        put_rows(right, right_rows(*scaled, norm_of(*za, C_CONTACT)))
        for q, v in enumerate(zb + [jnp.ones((8, W), F32)]):
            hi = v.astype(BF).astype(F32)
            lead[8 * q : 8 * q + 8, :] = hi
            lead[8 * (q + 8) : 8 * (q + 8) + 8, :] = v - hi
        for j in range(8):
            lhs = jnp.transpose(take_rows(feat, j)).astype(BF)
            kernel = gauss(lhs, take_rows(right, j).astype(BF))
            l16 = lead[pl.ds(j, 16, stride=8), :]
            both = jnp.concatenate([l16, jnp.where(upper, l16, 0.0)], axis=1).astype(BF)
            res = jnp.dot(both, two_halves(kernel), preferred_element_type=F32)
            acc[8 * j : 8 * j + 8, :] = res[0:8] + res[8:16]
        s = [acc[pl.ds(q, 8, stride=8), :] for q in range(4)]
        f = [STIFF * (za[q] * s[3] - s[q]) for q in range(3)]
        arm = [arm_ref[q, pl.ds(at, 8), :] for q in range(3)]
        t = [arm[1] * f[2] - arm[2] * f[1], arm[2] * f[0] - arm[0] * f[2],
             arm[0] * f[1] - arm[1] * f[0]]
        out_ref[pl.ds(at, 8), :] = columns_to_lanes([lane_sum(v) for v in f + t])
        return carry

    lax.fori_loop(0, clumps // 8, group, 0)


def contact(partner, arms, world, following):
    clumps = arms.shape[1]
    vm = pl.BlockSpec(memory_space=pltpu.VMEM)
    sm = pl.BlockSpec(memory_space=pltpu.SMEM)
    return pl.pallas_call(
        contact_kernel,
        out_shape=jax.ShapeDtypeStruct((clumps, W), F32),
        in_specs=[sm, vm, vm, vm],
        out_specs=vm,
        scratch_shapes=[
            pltpu.VMEM((3, 2 * clumps, W), F32),
            pltpu.VMEM((24, W), F32),
            pltpu.VMEM((FEATS * 8, W), F32),
            pltpu.VMEM((FEATS * 8, W), F32),
            pltpu.VMEM((W, W), F32),
            pltpu.VMEM((64, W), F32),
        ],
        compiler_params=pltpu.CompilerParams(vmem_limit_bytes=24 << 20),
        name="contact",
    )(partner, arms, world, following)


def fluid_kernel(first, ids_s, y_ref, table_ref, amp_ref, out_ref, right, acc):
    zero_tail(right)
    lane = lax.broadcasted_iota(jnp.int32, (8, W), 1)
    mine = (lane >> 4) == lax.broadcasted_iota(jnp.int32, (8, W), 0)
    place = lane & 15

    def group(g, carry):
        at = pl.multiple_of(g * 24, 8)
        y = [y_ref[pl.ds(at + 8 * q, 8), :] for q in range(3)]
        u = [v - 0.5 for v in y]
        scaled = [split3(v * (2.0 * C_FLUID)) for v in u]
        put_rows(right, right_rows(*scaled, norm_of(*u, C_FLUID)))
        valid = jnp.zeros((1, W), jnp.int32)
        for j in range(8):
            name = ids_s[g, first + j]
            valid = jnp.where((lane[0:1] >> 4) == j, name, valid)
            b = jnp.maximum(name, 0)
            kernel = gauss(table_ref[b], take_rows(right, j).astype(BF))
            res = jnp.dot(amp_ref[b], two_halves(kernel), preferred_element_type=F32)
            acc[8 * j : 8 * j + 8, :] = res[0:8] + res[8:16]
        s = [acc[pl.ds(q, 8, stride=8), :] for q in range(4)]
        cross = [y[1] * s[2] - y[2] * s[1], y[2] * s[0] - y[0] * s[2], y[0] * s[1] - y[1] * s[0]]
        moment = [y[q] * s[3] for q in range(3)]
        out = jnp.zeros((8, W), F32)
        for q, v in enumerate(s + cross + moment):
            out = jnp.where(place == q, lane_sum(v), out)
        row = jnp.sum(jnp.where(mine, out, 0.0), axis=0, keepdims=True)
        out_ref[pl.ds(g, 1), :] = jnp.where(valid >= 0, row, 0.0)
        return carry

    lax.fori_loop(0, out_ref.shape[0], group, 0)


def fluid(first, ids, spots, table, amp):
    vm = pl.BlockSpec(memory_space=pltpu.VMEM)
    sm = pl.BlockSpec(memory_space=pltpu.SMEM)
    return pl.pallas_call(
        functools.partial(fluid_kernel, first),
        out_shape=jax.ShapeDtypeStruct((W, W), F32),
        in_specs=[sm, vm, vm, vm],
        out_specs=vm,
        scratch_shapes=[pltpu.VMEM((FEATS * 8, W), F32), pltpu.VMEM((64, W), F32)],
        compiler_params=pltpu.CompilerParams(vmem_limit_bytes=24 << 20),
        name="fluid",
    )(ids, spots, table, amp)


def combine_kernel(dev_ref, rank_ref, off_ref, vel_ref, one_ref, two_ref, contact_ref, out_ref):
    entries = dev_ref.shape[1]
    clumps = entries // 2
    row = lax.broadcasted_iota(jnp.int32, (W, entries), 0)
    hot = (row == dev_ref[...]).astype(BF)
    rank = rank_ref[...]
    picked = jnp.zeros((16, entries), F32)
    for chunk, ref in enumerate((one_ref, two_ref)):
        spread = jnp.zeros((W, entries), F32)
        for part in split3(jnp.transpose(ref[...])):
            spread = spread + jnp.dot(part.astype(BF), hot, preferred_element_type=F32)
        spread = jnp.where((row >> 4) + 8 * chunk == rank, spread, 0.0)
        picked = picked + jnp.sum(spread.reshape(8, 16, entries), axis=0)
    touch = jnp.transpose(contact_ref[...])
    total = [touch[q : q + 1, :] for q in range(6)]
    v = [vel_ref[q : q + 1, :] for q in range(3)]
    for k in range(2):
        part = slice(k * clumps, k * clumps + clumps)
        g = [picked[q : q + 1, part] for q in range(10)]
        off = [off_ref[q : q + 1, part] for q in range(3)]
        f = [g[q] - v[q] * g[3] for q in range(3)]
        m = g[7:10]
        for q in range(3):
            a, b = (q + 1) % 3, (q + 2) % 3
            t = g[4 + q] - (m[a] * v[b] - m[b] * v[a]) - (off[a] * f[b] - off[b] * f[a])
            total[q] = total[q] + DRAG * f[q]
            total[3 + q] = total[3 + q] + DRAG * t
    for q in range(6):
        out_ref[q : q + 1, :] = total[q]


def combine(dev, rank, off, vel, one, two, touch):
    vm = pl.BlockSpec(memory_space=pltpu.VMEM)
    return pl.pallas_call(
        combine_kernel,
        out_shape=jax.ShapeDtypeStruct((6, vel.shape[1]), F32),
        in_specs=[vm] * 7,
        out_specs=vm,
        compiler_params=pltpu.CompilerParams(vmem_limit_bytes=24 << 20),
        name="combine",
    )(dev, rank, off, vel, one, two, touch)


def extended(cells, sides):
    for axis, dim in sides:
        count = lax.axis_size(axis)
        ends = count - 1
        head = lax.slice_in_dim(cells, 0, 1, axis=dim)
        tail = lax.slice_in_dim(cells, cells.shape[dim] - 1, cells.shape[dim], axis=dim)
        cells = jnp.concatenate(
            [
                lax.ppermute(tail, axis, [(i, (i + 1) % count) for i in range(ends)]),
                cells,
                lax.ppermute(head, axis, [((i + 1) % count, i) for i in range(ends)]),
            ],
            axis=dim,
        )
    return cells


def swap_all(array):
    return lax.all_to_all(array, AXES, split_axis=0, concat_axis=0, tiled=True)


def body(
    fluid_pos,
    fluid_vel,
    fluid_mass,
    fluid_count,
    clump_center,
    clump_vel,
    clump_arm,
    margin_device,
    margin_block,
    margin_offset,
    contact_partner,
):
    rows_x, rows_y, width = fluid_mass.shape
    blocks = rows_x * rows_y
    clumps = clump_arm.shape[0]
    entries = 2 * clumps
    devices = lax.axis_size(AXES)
    arms = jnp.transpose(clump_arm, (1, 0, 2))
    dev = margin_device.T.reshape(1, entries)
    blk = margin_block.T.reshape(1, entries)
    off = jnp.transpose(margin_offset, (2, 1, 0)).reshape(3, entries)
    vel = clump_vel.T
    first, second, ids, rank = prep(dev, blk, off, arms)
    names = swap_all(ids)
    got_first = swap_all(first.reshape(devices, 24, width))
    got_second = swap_all(second.reshape(devices, 24, width))
    world = arms + clump_center.T[:, :, None]
    following = lax.ppermute(world, AXES, [(i, (i + devices - 1) % devices) for i in range(devices)])
    touch = contact(contact_partner.reshape(1, clumps), arms, world, following)
    lanes = jnp.arange(width, dtype=jnp.int32)
    live = jnp.where(lanes[None, None, :] < fluid_count[..., None], fluid_mass, 0.0)
    planes = jnp.concatenate([jnp.moveaxis(fluid_pos, 2, 0), live[None]], axis=0)
    ext = extended(planes, (("stream", 1), ("span", 2)))
    ext = ext.reshape(4, (rows_x + 2) * (rows_y + 2), width)
    ext = jnp.pad(ext, ((0, 0), (0, 4), (0, 0)))
    own = planes.reshape(4, blocks, width)
    speed = jnp.moveaxis(fluid_vel, 2, 0).reshape(3, blocks, width)
    dens, table, amp = density(ext, own, fluid_mass.reshape(blocks, width), speed)
    one = swap_all(fluid(0, names, got_first.reshape(devices * 24, width), table, amp))
    two = swap_all(fluid(8, names, got_second.reshape(devices * 24, width), table, amp))
    loads = combine(dev, rank, off, vel, one, two, touch)
    return (dens.reshape(rows_x, rows_y, width), loads)


def solution(mesh):
    in_specs = (
        P("stream", "span", None, None),
        P("stream", "span", None, None),
        P("stream", "span", None),
        P("stream", "span"),
        P(("stream", "span"), None),
        P(("stream", "span"), None),
        P(("stream", "span"), None, None),
        P(("stream", "span"), None),
        P(("stream", "span"), None),
        P(("stream", "span"), None, None),
        P(("stream", "span")),
    )
    out_specs = (P("stream", "span", None), P(None, ("stream", "span")))
    return jax.shard_map(body, mesh=mesh, in_specs=in_specs, out_specs=out_specs, check_vma=False)
```

```python
import functools
import math

import jax
import jax.numpy as jnp
from jax import lax
from jax.experimental import pallas as pl
from jax.experimental.pallas import tpu as pltpu
from jax.sharding import PartitionSpec as P

H_SQ = 0.25
SIG_SQ = 0.5
DENS = 0.03125
DRAG = 0.002
STIFF = 0.005
LOG2E = math.log2(math.e)
C_FLUID = LOG2E / H_SQ
C_CONTACT = LOG2E / SIG_SQ
AXES = ("stream", "span")
W = 128
FEATS = 32
ROWS = 49
UNROLL = 4
DEAD = -30000.0
BF = jnp.bfloat16
F32 = jnp.float32


def split3(v):
    hi = v.astype(BF).astype(F32)
    rest = v - hi
    mid = rest.astype(BF).astype(F32)
    return hi, mid, rest - mid


def norm_of(x, y, z, coef):
    return (x * x + y * y + z * z) * (-coef)


def left_rows(xs, ys, zs, norm):
    h, m, low = ([c[i] for c in (xs, ys, zs)] for i in range(3))
    one = jnp.ones_like(h[0])
    return h + h + h + m + m + low + list(split3(norm)) + [one, one, one]


def right_rows(xs, ys, zs, norm):
    h, m, low = ([c[i] for c in (xs, ys, zs)] for i in range(3))
    one = jnp.ones_like(h[0])
    return h + m + low + h + m + h + [one, one, one] + list(split3(norm))


def put_rows(ref, rows, base=0):
    for i, row in enumerate(rows):
        ref[base + 8 * i : base + 8 * i + 8, :] = row


def zero_tail(ref, base=0):
    zero = jnp.zeros((8, W), F32)
    for i in range(24, FEATS):
        ref[base + 8 * i : base + 8 * i + 8, :] = zero


def take_rows(ref, j, base=0):
    return ref[pl.ds(base + j, FEATS, stride=8), :]


def gauss(left, right):
    return jnp.exp2(jnp.dot(left, right, preferred_element_type=F32))


def two_halves(kernel):
    hi = kernel.astype(BF)
    lo = (kernel - hi.astype(F32)).astype(BF)
    return jnp.concatenate([hi, lo], axis=0)


def lane_sum(v):
    return jnp.sum(v, axis=1, keepdims=True)


def prep_kernel(dev_ref, blk_ref, dev_s, off_s, arm_ref, send_ref, rank_ref, buf, rank_s, sems):
    entries = dev_ref.shape[1]
    parts = entries // W
    dev = dev_ref[...]
    row = lax.broadcasted_iota(jnp.int32, (W, entries), 0)
    hot = (row == dev).astype(F32)
    hot_b = hot.astype(BF)
    up = lax.broadcasted_iota(jnp.int32, (W, 2 * W), 0)
    lane = lax.broadcasted_iota(jnp.int32, (W, 2 * W), 1)
    tri = jnp.where(lane >= W, 1.0, jnp.where(up < lane, 1.0, 0.0)).astype(BF)
    carry = jnp.zeros((W, W), F32)
    ranks = []
    for part in range(parts):
        piece = slice(part * W, part * W + W)
        both = jnp.dot(hot_b[:, piece], tri, preferred_element_type=F32)
        ranks.append(jnp.sum(hot[:, piece] * (both[:, :W] + carry), axis=0, keepdims=True))
        carry = carry + both[:, W:]
    rank = jnp.concatenate(ranks, axis=1).astype(jnp.int32)
    rank_ref[...] = rank
    move = pltpu.make_async_copy(rank_ref, rank_s, sems.at[0])
    move.start()
    named = jnp.where(row == rank, blk_ref[...] + 1, 0).astype(F32).astype(BF)
    ids = lax.dot_general(hot_b, named, (((1,), (1,)), ((), ())), preferred_element_type=F32)
    for d in range(W):
        buf[d * ROWS + 48 : d * ROWS + 49, :] = ids[d : d + 1, :]
    move.wait()

    clumps = entries // 2

    def step(i, carry):
        for k in range(2):
            for j in range(8):
                c = i * 8 + j
                e = k * clumps + c
                base = dev_s[0, e] * ROWS + rank_s[0, e]
                for q in range(3):
                    buf[pl.ds(base + 16 * q, 1), :] = (
                        arm_ref[q, pl.ds(c, 1), :] + off_s[q, e]
                    )
        return carry

    lax.fori_loop(0, clumps // 8, step, 0)
    out = pltpu.make_async_copy(buf, send_ref, sems.at[0])
    out.start()
    out.wait()


def prep(dev, blk, off, arms):
    entries = dev.shape[1]
    vm = pl.BlockSpec(memory_space=pltpu.VMEM)
    sm = pl.BlockSpec(memory_space=pltpu.SMEM)
    hbm = pl.BlockSpec(memory_space=pl.ANY)
    return pl.pallas_call(
        prep_kernel,
        out_shape=(
            jax.ShapeDtypeStruct((W * ROWS, W), F32),
            jax.ShapeDtypeStruct((1, entries), jnp.int32),
        ),
        in_specs=[vm, vm, sm, sm, vm],
        out_specs=(hbm, vm),
        scratch_shapes=[
            pltpu.VMEM((W * ROWS, W), F32),
            pltpu.SMEM((1, entries), jnp.int32),
            pltpu.SemaphoreType.DMA((1,)),
        ],
        compiler_params=pltpu.CompilerParams(vmem_limit_bytes=24 << 20),
        name="prep",
    )(dev, blk, dev, off, arms)


def density_kernel(ext_ref, own_ref, mass_ref, vel_ref, dens_ref, table_ref, amp_ref,
                   feat, right, sums, left, wide):
    rows_y = 8
    zero_tail(feat)
    for s in range(9):
        zero_tail(right, s * FEATS * 8)

    def coords(ref, at):
        return [ref[q, pl.ds(at, 8), :] - 0.5 for q in range(3)]

    def ext_group(g, carry):
        at = pl.multiple_of(g * 8, 8)
        x, y, z = coords(ext_ref, at)
        m = ext_ref[3, pl.ds(at, 8), :]
        logm = jnp.where(m > 0.0, jnp.log2(jnp.where(m > 0.0, m, 1.0)), DEAD)
        norm = norm_of(x, y, z, C_FLUID) + logm
        put_rows(feat, left_rows(split3(x), split3(y), split3(z), norm))
        for j in range(8):
            left[at + j] = jnp.transpose(take_rows(feat, j)).astype(BF)
        return carry

    lax.fori_loop(0, ext_ref.shape[1] // 8, ext_group, 0)

    def own_row(a, carry):
        at = pl.multiple_of(a * 8, 8)
        x, y, z = coords(own_ref, at)
        xs = [x + 1.0, x, x - 1.0]
        ys = [y + 1.0, y, y - 1.0]
        scale = 2.0 * C_FLUID
        xsplit = [split3(v * scale) for v in xs]
        ysplit = [split3(v * scale) for v in ys]
        zsplit = split3(z * scale)
        for ix in range(3):
            for iy in range(3):
                norm = norm_of(xs[ix], ys[iy], z, C_FLUID)
                put_rows(right, right_rows(xsplit[ix], ysplit[iy], zsplit, norm),
                         (ix * 3 + iy) * FEATS * 8)

        def block(b, inner):
            total = jnp.zeros((8, W), F32)
            for ix in range(3):
                for iy in range(3):
                    rhs = take_rows(right, b, (ix * 3 + iy) * FEATS * 8).astype(BF)
                    lhs = left[(a + ix) * 10 + b + iy]
                    total = total + jnp.sum(gauss(lhs, rhs).reshape(16, 8, W), axis=0)
            sums[pl.ds(b, 1), :] = jnp.sum(total, axis=0, keepdims=True)
            return inner

        lax.fori_loop(0, rows_y, block, 0, unroll=4)
        density = DENS * (mass_ref[pl.ds(at, 8), :] + sums[...])
        dens_ref[pl.ds(at, 8), :] = density
        weight = own_ref[3, pl.ds(at, 8), :] / density
        parts = [vel_ref[q, pl.ds(at, 8), :] * weight for q in range(3)] + [weight]
        zero = jnp.zeros((8, W), F32)
        for q, v in enumerate(parts):
            hi = v.astype(BF).astype(F32)
            wide[8 * q : 8 * q + 8, :] = hi
            wide[8 * (q + 8) : 8 * (q + 8) + 8, :] = v - hi
        for q in (4, 5, 6, 7, 12, 13, 14, 15):
            wide[8 * q : 8 * q + 8, :] = zero
        norm = norm_of(x, y, z, C_FLUID)
        put_rows(feat, left_rows(split3(x), split3(y), split3(z), norm))
        upper = lax.broadcasted_iota(jnp.int32, (16, W), 0) < 8
        for j in range(8):
            table_ref[at + j] = jnp.transpose(take_rows(feat, j)).astype(BF)
            a16 = wide[pl.ds(j, 16, stride=8), :]
            amp_ref[at + j, :, 0:W] = a16.astype(BF)
            amp_ref[at + j, :, W : 2 * W] = jnp.where(upper, a16, 0.0).astype(BF)
        return carry

    lax.fori_loop(0, 8, own_row, 0)


def density(ext, own, mass, vel):
    blocks = mass.shape[0]
    vm = pl.BlockSpec(memory_space=pltpu.VMEM)
    return pl.pallas_call(
        density_kernel,
        out_shape=(
            jax.ShapeDtypeStruct((blocks, W), F32),
            jax.ShapeDtypeStruct((blocks, W, FEATS), BF),
            jax.ShapeDtypeStruct((blocks, 16, 2 * W), BF),
        ),
        in_specs=[vm] * 4,
        out_specs=(vm, vm, vm),
        scratch_shapes=[
            pltpu.VMEM((FEATS * 8, W), F32),
            pltpu.VMEM((9 * FEATS * 8, W), F32),
            pltpu.VMEM((8, W), F32),
            pltpu.VMEM((ext.shape[1], W, FEATS), BF),
            pltpu.VMEM((W, W), F32),
        ],
        compiler_params=pltpu.CompilerParams(vmem_limit_bytes=24 << 20),
        name="density",
    )(ext, own, mass, vel)


def columns_to_lanes(cols):
    lane = lax.broadcasted_iota(jnp.int32, (8, W), 1)
    out = jnp.zeros((8, W), F32)
    for q, col in enumerate(cols):
        out = jnp.where(lane == q, col, out)
    return out


def contact_kernel(partner_s, arm_ref, world_ref, next_ref, out_ref, cand, gat, feat, right, lead, acc):
    clumps = arm_ref.shape[1]
    cand[:, 0:clumps, :] = world_ref[...]
    cand[:, clumps : 2 * clumps, :] = next_ref[...]
    zero = jnp.zeros((8, W), F32)
    for t in range(UNROLL):
        zero_tail(feat, t * FEATS * 8)
        zero_tail(right, t * FEATS * 8)
        for q in (4, 5, 6, 7, 12, 13, 14, 15):
            lead[t * W + 8 * q : t * W + 8 * q + 8, :] = zero
    upper = lax.broadcasted_iota(jnp.int32, (16, W), 0) < 8

    def group(i, carry):
        zas, ats = [], []
        for t in range(UNROLL):
            at = pl.multiple_of((i * UNROLL + t) * 8, 8)
            ats.append(at)
            for j in range(8):
                p = partner_s[0, at + j]
                for q in range(3):
                    spot = 24 * t + 8 * q + j
                    gat[spot : spot + 1, :] = cand[q, pl.ds(p, 1), :]
            za = [world_ref[q, pl.ds(at, 8), :] - 0.5 for q in range(3)]
            zas.append(za)
            scaled = [split3(v * (2.0 * C_CONTACT)) for v in za]
            put_rows(right, right_rows(*scaled, norm_of(*za, C_CONTACT)), t * FEATS * 8)
        for t in range(UNROLL):
            zb = [gat[24 * t + 8 * q : 24 * t + 8 * q + 8, :] - 0.5 for q in range(3)]
            parts = [split3(v) for v in zb]
            put_rows(feat, left_rows(*parts, norm_of(*zb, C_CONTACT)), t * FEATS * 8)
            for q, v in enumerate(zb + [jnp.ones((8, W), F32)]):
                hi = v.astype(BF).astype(F32)
                spot = t * W + 8 * q
                lead[spot : spot + 8, :] = hi
                lead[spot + 64 : spot + 72, :] = v - hi
        for t in range(UNROLL):
            for j in range(8):
                lhs = jnp.transpose(take_rows(feat, j, t * FEATS * 8)).astype(BF)
                kernel = gauss(lhs, take_rows(right, j, t * FEATS * 8).astype(BF))
                l16 = lead[pl.ds(t * W + j, 16, stride=8), :]
                both = jnp.concatenate([l16, jnp.where(upper, l16, 0.0)], axis=1).astype(BF)
                res = jnp.dot(both, two_halves(kernel), preferred_element_type=F32)
                spot = 64 * t + 8 * j
                acc[spot : spot + 8, :] = res[0:8] + res[8:16]
        for t in range(UNROLL):
            at, za = ats[t], zas[t]
            s = [acc[pl.ds(64 * t + q, 8, stride=8), :] for q in range(4)]
            f = [STIFF * (za[q] * s[3] - s[q]) for q in range(3)]
            arm = [arm_ref[q, pl.ds(at, 8), :] for q in range(3)]
            tq = [arm[1] * f[2] - arm[2] * f[1], arm[2] * f[0] - arm[0] * f[2],
                  arm[0] * f[1] - arm[1] * f[0]]
            out_ref[pl.ds(at, 8), :] = columns_to_lanes([lane_sum(v) for v in f + tq])
        return carry

    lax.fori_loop(0, clumps // (8 * UNROLL), group, 0)


def contact(partner, arms, world, following):
    clumps = arms.shape[1]
    vm = pl.BlockSpec(memory_space=pltpu.VMEM)
    sm = pl.BlockSpec(memory_space=pltpu.SMEM)
    return pl.pallas_call(
        contact_kernel,
        out_shape=jax.ShapeDtypeStruct((clumps, W), F32),
        in_specs=[sm, vm, vm, vm],
        out_specs=vm,
        scratch_shapes=[
            pltpu.VMEM((3, 2 * clumps, W), F32),
            pltpu.VMEM((UNROLL * 24, W), F32),
            pltpu.VMEM((UNROLL * FEATS * 8, W), F32),
            pltpu.VMEM((UNROLL * FEATS * 8, W), F32),
            pltpu.VMEM((UNROLL * W, W), F32),
            pltpu.VMEM((UNROLL * 64, W), F32),
        ],
        compiler_params=pltpu.CompilerParams(vmem_limit_bytes=24 << 20),
        name="contact",
    )(partner, arms, world, following)


def fluid_kernel(y_ref, table_ref, amp_ref, out_ref, names, names_s, right, acc, sems):
    for t in range(2 * UNROLL):
        zero_tail(right, t * FEATS * 8)
    lane = lax.broadcasted_iota(jnp.int32, (8, W), 1)
    mine = (lane >> 4) == lax.broadcasted_iota(jnp.int32, (8, W), 0)
    place = lane & 15
    devices = out_ref.shape[0] // 2

    def read(g, carry):
        names[pl.ds(g, 1), :] = y_ref[pl.ds(g * ROWS + 48, 1), :].astype(jnp.int32) - 1
        return carry

    lax.fori_loop(0, devices, read, 0, unroll=8)
    move = pltpu.make_async_copy(names, names_s, sems.at[0])
    move.start()
    move.wait()

    def group(i, carry):
        ys, valids = [], []
        for t in range(2 * UNROLL):
            g = i * UNROLL + t // 2
            at = g * ROWS + (t % 2) * 8
            y = [y_ref[pl.ds(at + 16 * q, 8), :] for q in range(3)]
            ys.append(y)
            u = [v - 0.5 for v in y]
            scaled = [split3(v * (2.0 * C_FLUID)) for v in u]
            put_rows(right, right_rows(*scaled, norm_of(*u, C_FLUID)), t * FEATS * 8)
        for t in range(2 * UNROLL):
            g = i * UNROLL + t // 2
            valid = jnp.zeros((1, W), jnp.int32)
            for j in range(8):
                name = names_s[g, (t % 2) * 8 + j]
                valid = jnp.where((lane[0:1] >> 4) == j, name, valid)
                b = jnp.maximum(name, 0)
                kernel = gauss(table_ref[b], take_rows(right, j, t * FEATS * 8).astype(BF))
                res = jnp.dot(amp_ref[b], two_halves(kernel), preferred_element_type=F32)
                spot = 64 * t + 8 * j
                acc[spot : spot + 8, :] = res[0:8] + res[8:16]
            valids.append(valid)
        for t in range(2 * UNROLL):
            g = i * UNROLL + t // 2
            y = ys[t]
            s = [acc[pl.ds(64 * t + q, 8, stride=8), :] for q in range(4)]
            cross = [y[1] * s[2] - y[2] * s[1], y[2] * s[0] - y[0] * s[2],
                     y[0] * s[1] - y[1] * s[0]]
            moment = [y[q] * s[3] for q in range(3)]
            out = jnp.zeros((8, W), F32)
            for q, v in enumerate(s + cross + moment):
                out = jnp.where(place == q, lane_sum(v), out)
            row = jnp.sum(jnp.where(mine, out, 0.0), axis=0, keepdims=True)
            out_ref[pl.ds(2 * g + t % 2, 1), :] = jnp.where(valids[t] >= 0, row, 0.0)
        return carry

    lax.fori_loop(0, devices // UNROLL, group, 0)


def fluid(spots, table, amp):
    vm = pl.BlockSpec(memory_space=pltpu.VMEM)
    return pl.pallas_call(
        fluid_kernel,
        out_shape=jax.ShapeDtypeStruct((2 * W, W), F32),
        in_specs=[vm, vm, vm],
        out_specs=vm,
        scratch_shapes=[
            pltpu.VMEM((W, W), jnp.int32),
            pltpu.SMEM((W, W), jnp.int32),
            pltpu.VMEM((2 * UNROLL * FEATS * 8, W), F32),
            pltpu.VMEM((2 * UNROLL * 64, W), F32),
            pltpu.SemaphoreType.DMA((1,)),
        ],
        compiler_params=pltpu.CompilerParams(vmem_limit_bytes=24 << 20),
        name="fluid",
    )(spots, table, amp)


def combine_kernel(dev_ref, rank_ref, off_ref, vel_ref, got_ref, contact_ref, out_ref):
    entries = dev_ref.shape[1]
    clumps = entries // 2
    row = lax.broadcasted_iota(jnp.int32, (W, entries), 0)
    hot = (row == dev_ref[...]).astype(BF)
    rank = rank_ref[...]
    picked = jnp.zeros((16, entries), F32)
    for chunk in range(2):
        spread = jnp.zeros((W, entries), F32)
        for part in split3(jnp.transpose(got_ref[pl.ds(chunk, W, stride=2), :])):
            spread = spread + jnp.dot(part.astype(BF), hot, preferred_element_type=F32)
        spread = jnp.where((row >> 4) + 8 * chunk == rank, spread, 0.0)
        picked = picked + jnp.sum(spread.reshape(8, 16, entries), axis=0)
    touch = jnp.transpose(contact_ref[...])
    total = [touch[q : q + 1, :] for q in range(6)]
    v = [vel_ref[q : q + 1, :] for q in range(3)]
    for k in range(2):
        part = slice(k * clumps, k * clumps + clumps)
        g = [picked[q : q + 1, part] for q in range(10)]
        off = [off_ref[q : q + 1, part] for q in range(3)]
        f = [g[q] - v[q] * g[3] for q in range(3)]
        m = g[7:10]
        for q in range(3):
            a, b = (q + 1) % 3, (q + 2) % 3
            t = g[4 + q] - (m[a] * v[b] - m[b] * v[a]) - (off[a] * f[b] - off[b] * f[a])
            total[q] = total[q] + DRAG * f[q]
            total[3 + q] = total[3 + q] + DRAG * t
    for q in range(6):
        out_ref[q : q + 1, :] = total[q]


def combine(dev, rank, off, vel, got, touch):
    vm = pl.BlockSpec(memory_space=pltpu.VMEM)
    return pl.pallas_call(
        combine_kernel,
        out_shape=jax.ShapeDtypeStruct((6, vel.shape[1]), F32),
        in_specs=[vm] * 6,
        out_specs=vm,
        compiler_params=pltpu.CompilerParams(vmem_limit_bytes=24 << 20),
        name="combine",
    )(dev, rank, off, vel, got, touch)


def extended(cells, sides):
    for axis, dim in sides:
        count = lax.axis_size(axis)
        ends = count - 1
        head = lax.slice_in_dim(cells, 0, 1, axis=dim)
        tail = lax.slice_in_dim(cells, cells.shape[dim] - 1, cells.shape[dim], axis=dim)
        cells = jnp.concatenate(
            [
                lax.ppermute(tail, axis, [(i, (i + 1) % count) for i in range(ends)]),
                cells,
                lax.ppermute(head, axis, [((i + 1) % count, i) for i in range(ends)]),
            ],
            axis=dim,
        )
    return cells


def swap_all(array):
    return lax.all_to_all(array, AXES, split_axis=0, concat_axis=0, tiled=True)


def body(
    fluid_pos,
    fluid_vel,
    fluid_mass,
    fluid_count,
    clump_center,
    clump_vel,
    clump_arm,
    margin_device,
    margin_block,
    margin_offset,
    contact_partner,
):
    rows_x, rows_y, width = fluid_mass.shape
    blocks = rows_x * rows_y
    clumps = clump_arm.shape[0]
    entries = 2 * clumps
    devices = lax.axis_size(AXES)
    arms = jnp.transpose(clump_arm, (1, 0, 2))
    dev = margin_device.T.reshape(1, entries)
    blk = margin_block.T.reshape(1, entries)
    off = jnp.transpose(margin_offset, (2, 1, 0)).reshape(3, entries)
    vel = clump_vel.T
    send, rank = prep(dev, blk, off, arms)
    got = swap_all(send.reshape(devices, 1, ROWS * width))
    world = arms + clump_center.T[:, :, None]
    following = lax.ppermute(world, AXES, [(i, (i + devices - 1) % devices) for i in range(devices)])
    touch = contact(contact_partner.reshape(1, clumps), arms, world, following)
    lanes = jnp.arange(width, dtype=jnp.int32)
    live = jnp.where(lanes[None, None, :] < fluid_count[..., None], fluid_mass, 0.0)
    planes = jnp.concatenate([jnp.moveaxis(fluid_pos, 2, 0), live[None]], axis=0)
    ext = extended(planes, (("stream", 1), ("span", 2)))
    ext = ext.reshape(4, (rows_x + 2) * (rows_y + 2), width)
    ext = jnp.pad(ext, ((0, 0), (0, 4), (0, 0)))
    own = planes.reshape(4, blocks, width)
    speed = jnp.moveaxis(fluid_vel, 2, 0).reshape(3, blocks, width)
    dens, table, amp = density(ext, own, fluid_mass.reshape(blocks, width), speed)
    got, touch = lax.optimization_barrier((got, touch))
    sums = fluid(got.reshape(devices * ROWS, width), table, amp)
    back = swap_all(sums.reshape(devices, 1, 2 * width)).reshape(2 * devices, width)
    loads = combine(dev, rank, off, vel, back, touch)
    return (dens.reshape(rows_x, rows_y, width), loads)


def solution(mesh):
    in_specs = (
        P("stream", "span", None, None),
        P("stream", "span", None, None),
        P("stream", "span", None),
        P("stream", "span"),
        P(("stream", "span"), None),
        P(("stream", "span"), None),
        P(("stream", "span"), None, None),
        P(("stream", "span"), None),
        P(("stream", "span"), None),
        P(("stream", "span"), None, None),
        P(("stream", "span")),
    )
    out_specs = (P("stream", "span", None), P(None, ("stream", "span")))
    return jax.shard_map(body, mesh=mesh, in_specs=in_specs, out_specs=out_specs, check_vma=False)
```

```python
import functools
import math

import jax
import jax.numpy as jnp
from jax import lax
from jax.experimental import pallas as pl
from jax.experimental.pallas import tpu as pltpu
from jax.sharding import PartitionSpec as P

H_SQ = 0.25
SIG_SQ = 0.5
DENS = 0.03125
DRAG = 0.002
STIFF = 0.005
LOG2E = math.log2(math.e)
C_FLUID = LOG2E / H_SQ
C_CONTACT = LOG2E / SIG_SQ
AXES = ("stream", "span")
W = 128
FEATS = 32
ROWS = 25
UNROLL = 4
GROUPS = 8
DEAD = -30000.0
BF = jnp.bfloat16
F32 = jnp.float32


def split3(v):
    hi = v.astype(BF).astype(F32)
    rest = v - hi
    mid = rest.astype(BF).astype(F32)
    return hi, mid, rest - mid


def norm_of(x, y, z, coef):
    return (x * x + y * y + z * z) * (-coef)


def left_rows(xs, ys, zs, norm):
    h, m, low = ([c[i] for c in (xs, ys, zs)] for i in range(3))
    one = jnp.ones_like(h[0])
    return h + h + h + m + m + low + list(split3(norm)) + [one, one, one]


def right_rows(xs, ys, zs, norm):
    h, m, low = ([c[i] for c in (xs, ys, zs)] for i in range(3))
    one = jnp.ones_like(h[0])
    return h + m + low + h + m + h + [one, one, one] + list(split3(norm))


def put_rows(ref, rows, base=0):
    for i, row in enumerate(rows):
        ref[base + 8 * i : base + 8 * i + 8, :] = row


def zero_tail(ref, base=0):
    zero = jnp.zeros((8, W), F32)
    for i in range(24, FEATS):
        ref[base + 8 * i : base + 8 * i + 8, :] = zero


def take_rows(ref, j, base=0):
    return ref[pl.ds(base + j, FEATS, stride=8), :]


def gauss(left, right):
    return jnp.exp2(jnp.dot(left, right, preferred_element_type=F32))


def two_halves(kernel):
    hi = kernel.astype(BF)
    lo = (kernel - hi.astype(F32)).astype(BF)
    return jnp.concatenate([hi, lo], axis=0)


def lane_sum(v):
    return jnp.sum(v, axis=1, keepdims=True)


def prep_kernel(dev_ref, blk_ref, dev_s, off_s, arm_ref, first_ref, second_ref, rank_ref, buf, rank_s, sems):
    entries = dev_ref.shape[1]
    parts = entries // W
    dev = dev_ref[...]
    row = lax.broadcasted_iota(jnp.int32, (W, entries), 0)
    hot = (row == dev).astype(F32)
    hot_b = hot.astype(BF)
    up = lax.broadcasted_iota(jnp.int32, (W, 2 * W), 0)
    lane = lax.broadcasted_iota(jnp.int32, (W, 2 * W), 1)
    tri = jnp.where(lane >= W, 1.0, jnp.where(up < lane, 1.0, 0.0)).astype(BF)
    carry = jnp.zeros((W, W), F32)
    ranks = []
    for part in range(parts):
        piece = slice(part * W, part * W + W)
        both = jnp.dot(hot_b[:, piece], tri, preferred_element_type=F32)
        ranks.append(jnp.sum(hot[:, piece] * (both[:, :W] + carry), axis=0, keepdims=True))
        carry = carry + both[:, W:]
    rank = jnp.concatenate(ranks, axis=1).astype(jnp.int32)
    rank_ref[...] = rank
    move = pltpu.make_async_copy(rank_ref, rank_s, sems.at[0])
    move.start()
    named = jnp.where(row == rank, blk_ref[...] + 1, 0).astype(F32).astype(BF)
    ids = lax.dot_general(hot_b, named, (((1,), (1,)), ((), ())), preferred_element_type=F32)
    late = pltpu.roll(ids, W - 8, 1)
    for d in range(W):
        for part, rows in enumerate((ids, late)):
            spot = (part * W + d) * ROWS + 24
            buf[spot : spot + 1, :] = rows[d : d + 1, :]
    move.wait()

    clumps = entries // 2

    def step(i, carry):
        for k in range(2):
            for j in range(8):
                c = i * 8 + j
                e = k * clumps + c
                r = rank_s[0, e]
                base = ((r >> 3) * W + dev_s[0, e]) * ROWS + (r & 7)
                for q in range(3):
                    buf[pl.ds(base + 8 * q, 1), :] = (
                        arm_ref[q, pl.ds(c, 1), :] + off_s[q, e]
                    )
        return carry

    lax.fori_loop(0, clumps // 8, step, 0)
    half = W * ROWS
    one = pltpu.make_async_copy(buf.at[pl.ds(0, half)], first_ref, sems.at[0])
    two = pltpu.make_async_copy(buf.at[pl.ds(half, half)], second_ref, sems.at[1])
    one.start()
    two.start()
    one.wait()
    two.wait()


def prep(dev, blk, off, arms):
    entries = dev.shape[1]
    vm = pl.BlockSpec(memory_space=pltpu.VMEM)
    sm = pl.BlockSpec(memory_space=pltpu.SMEM)
    hbm = pl.BlockSpec(memory_space=pltpu.HBM)
    send = jax.ShapeDtypeStruct((W * ROWS, W), F32)
    return pl.pallas_call(
        prep_kernel,
        out_shape=(send, send, jax.ShapeDtypeStruct((1, entries), jnp.int32)),
        in_specs=[vm, vm, sm, sm, vm],
        out_specs=(hbm, hbm, vm),
        scratch_shapes=[
            pltpu.VMEM((2 * W * ROWS, W), F32),
            pltpu.SMEM((1, entries), jnp.int32),
            pltpu.SemaphoreType.DMA((2,)),
        ],
        compiler_params=pltpu.CompilerParams(vmem_limit_bytes=16 << 20),
        name="prep",
    )(dev, blk, dev, off, arms)


def density_kernel(ext_ref, own_ref, mass_ref, vel_ref, dens_ref, table_ref, amp_ref,
                   feat, right, sums, left, wide):
    rows_y = 8
    zero_tail(feat)
    for s in range(9):
        zero_tail(right, s * FEATS * 8)

    def coords(ref, at):
        return [ref[q, pl.ds(at, 8), :] - 0.5 for q in range(3)]

    def ext_group(g, carry):
        at = pl.multiple_of(g * 8, 8)
        x, y, z = coords(ext_ref, at)
        m = ext_ref[3, pl.ds(at, 8), :]
        logm = jnp.where(m > 0.0, jnp.log2(jnp.where(m > 0.0, m, 1.0)), DEAD)
        norm = norm_of(x, y, z, C_FLUID) + logm
        put_rows(feat, left_rows(split3(x), split3(y), split3(z), norm))
        for j in range(8):
            left[at + j] = jnp.transpose(take_rows(feat, j)).astype(BF)
        return carry

    lax.fori_loop(0, ext_ref.shape[1] // 8, ext_group, 0)

    def own_row(a, carry):
        at = pl.multiple_of(a * 8, 8)
        x, y, z = coords(own_ref, at)
        xs = [x + 1.0, x, x - 1.0]
        ys = [y + 1.0, y, y - 1.0]
        scale = 2.0 * C_FLUID
        xsplit = [split3(v * scale) for v in xs]
        ysplit = [split3(v * scale) for v in ys]
        zsplit = split3(z * scale)
        for ix in range(3):
            for iy in range(3):
                norm = norm_of(xs[ix], ys[iy], z, C_FLUID)
                put_rows(right, right_rows(xsplit[ix], ysplit[iy], zsplit, norm),
                         (ix * 3 + iy) * FEATS * 8)

        def block(b, inner):
            total = jnp.zeros((8, W), F32)
            for ix in range(3):
                for iy in range(3):
                    rhs = take_rows(right, b, (ix * 3 + iy) * FEATS * 8).astype(BF)
                    lhs = left[(a + ix) * 10 + b + iy]
                    total = total + jnp.sum(gauss(lhs, rhs).reshape(16, 8, W), axis=0)
            sums[pl.ds(b, 1), :] = jnp.sum(total, axis=0, keepdims=True)
            return inner

        lax.fori_loop(0, rows_y, block, 0, unroll=4)
        density = DENS * (mass_ref[pl.ds(at, 8), :] + sums[...])
        dens_ref[pl.ds(at, 8), :] = density
        weight = own_ref[3, pl.ds(at, 8), :] / density
        parts = [vel_ref[q, pl.ds(at, 8), :] * weight for q in range(3)] + [weight]
        zero = jnp.zeros((8, W), F32)
        for q, v in enumerate(parts):
            hi = v.astype(BF).astype(F32)
            wide[8 * q : 8 * q + 8, :] = hi
            wide[8 * (q + 8) : 8 * (q + 8) + 8, :] = v - hi
        for q in (4, 5, 6, 7, 12, 13, 14, 15):
            wide[8 * q : 8 * q + 8, :] = zero
        norm = norm_of(x, y, z, C_FLUID)
        put_rows(feat, left_rows(split3(x), split3(y), split3(z), norm))
        upper = lax.broadcasted_iota(jnp.int32, (16, W), 0) < 8
        for j in range(8):
            table_ref[at + j] = jnp.transpose(take_rows(feat, j)).astype(BF)
            a16 = wide[pl.ds(j, 16, stride=8), :]
            amp_ref[at + j, :, 0:W] = a16.astype(BF)
            amp_ref[at + j, :, W : 2 * W] = jnp.where(upper, a16, 0.0).astype(BF)
        return carry

    lax.fori_loop(0, 8, own_row, 0)


def density(ext, own, mass, vel):
    blocks = mass.shape[0]
    vm = pl.BlockSpec(memory_space=pltpu.VMEM)
    return pl.pallas_call(
        density_kernel,
        out_shape=(
            jax.ShapeDtypeStruct((blocks, W), F32),
            jax.ShapeDtypeStruct((blocks, W, FEATS), BF),
            jax.ShapeDtypeStruct((blocks, 16, 2 * W), BF),
        ),
        in_specs=[vm] * 4,
        out_specs=(vm, vm, vm),
        scratch_shapes=[
            pltpu.VMEM((FEATS * 8, W), F32),
            pltpu.VMEM((9 * FEATS * 8, W), F32),
            pltpu.VMEM((8, W), F32),
            pltpu.VMEM((ext.shape[1], W, FEATS), BF),
            pltpu.VMEM((W, W), F32),
        ],
        compiler_params=pltpu.CompilerParams(vmem_limit_bytes=14 << 20),
        name="density",
    )(ext, own, mass, vel)


def columns_to_lanes(cols):
    lane = lax.broadcasted_iota(jnp.int32, (8, W), 1)
    out = jnp.zeros((8, W), F32)
    for q, col in enumerate(cols):
        out = jnp.where(lane == q, col, out)
    return out


def contact_kernel(partner_s, arm_ref, world_ref, next_ref, after_ref, out_ref, done_ref, cand, gat, feat, right, lead, acc):
    clumps = arm_ref.shape[1]
    done_ref[...] = jnp.zeros_like(done_ref)
    cand[:, 0:clumps, :] = world_ref[...]
    cand[:, clumps : 2 * clumps, :] = next_ref[...]
    zero = jnp.zeros((8, W), F32)
    for t in range(UNROLL):
        zero_tail(feat, t * FEATS * 8)
        zero_tail(right, t * FEATS * 8)
        for q in (4, 5, 6, 7, 12, 13, 14, 15):
            lead[t * W + 8 * q : t * W + 8 * q + 8, :] = zero
    upper = lax.broadcasted_iota(jnp.int32, (16, W), 0) < 8

    def group(i, carry):
        zas, ats = [], []
        for t in range(UNROLL):
            at = pl.multiple_of((i * UNROLL + t) * 8, 8)
            ats.append(at)
            for j in range(8):
                p = partner_s[0, at + j]
                for q in range(3):
                    spot = 24 * t + 8 * q + j
                    gat[spot : spot + 1, :] = cand[q, pl.ds(p, 1), :]
            za = [world_ref[q, pl.ds(at, 8), :] - 0.5 for q in range(3)]
            zas.append(za)
            scaled = [split3(v * (2.0 * C_CONTACT)) for v in za]
            put_rows(right, right_rows(*scaled, norm_of(*za, C_CONTACT)), t * FEATS * 8)
        for t in range(UNROLL):
            zb = [gat[24 * t + 8 * q : 24 * t + 8 * q + 8, :] - 0.5 for q in range(3)]
            parts = [split3(v) for v in zb]
            put_rows(feat, left_rows(*parts, norm_of(*zb, C_CONTACT)), t * FEATS * 8)
            for q, v in enumerate(zb + [jnp.ones((8, W), F32)]):
                hi = v.astype(BF).astype(F32)
                spot = t * W + 8 * q
                lead[spot : spot + 8, :] = hi
                lead[spot + 64 : spot + 72, :] = v - hi
        for t in range(UNROLL):
            for j in range(8):
                lhs = jnp.transpose(take_rows(feat, j, t * FEATS * 8)).astype(BF)
                kernel = gauss(lhs, take_rows(right, j, t * FEATS * 8).astype(BF))
                l16 = lead[pl.ds(t * W + j, 16, stride=8), :]
                both = jnp.concatenate([l16, jnp.where(upper, l16, 0.0)], axis=1).astype(BF)
                res = jnp.dot(both, two_halves(kernel), preferred_element_type=F32)
                spot = 64 * t + 8 * j
                acc[spot : spot + 8, :] = res[0:8] + res[8:16]
        for t in range(UNROLL):
            at, za = ats[t], zas[t]
            s = [acc[pl.ds(64 * t + q, 8, stride=8), :] for q in range(4)]
            f = [STIFF * (za[q] * s[3] - s[q]) for q in range(3)]
            arm = [arm_ref[q, pl.ds(at, 8), :] for q in range(3)]
            tq = [arm[1] * f[2] - arm[2] * f[1], arm[2] * f[0] - arm[0] * f[2],
                  arm[0] * f[1] - arm[1] * f[0]]
            out_ref[pl.ds(at, 8), :] = columns_to_lanes([lane_sum(v) for v in f + tq])
        return carry

    lax.fori_loop(0, clumps // (8 * UNROLL), group, 0)


def contact(partner, arms, world, following, after):
    clumps = arms.shape[1]
    vm = pl.BlockSpec(memory_space=pltpu.VMEM)
    sm = pl.BlockSpec(memory_space=pltpu.SMEM)
    return pl.pallas_call(
        contact_kernel,
        out_shape=(jax.ShapeDtypeStruct((clumps, W), F32), jax.ShapeDtypeStruct((8, W), F32)),
        in_specs=[sm, vm, vm, vm, pl.BlockSpec(memory_space=pl.ANY)],
        out_specs=(vm, vm),
        scratch_shapes=[
            pltpu.VMEM((3, 2 * clumps, W), F32),
            pltpu.VMEM((UNROLL * 24, W), F32),
            pltpu.VMEM((UNROLL * FEATS * 8, W), F32),
            pltpu.VMEM((UNROLL * FEATS * 8, W), F32),
            pltpu.VMEM((UNROLL * W, W), F32),
            pltpu.VMEM((UNROLL * 64, W), F32),
        ],
        compiler_params=pltpu.CompilerParams(vmem_limit_bytes=10 << 20),
        name="contact",
    )(partner, arms, world, following, after)


def fluid_kernel(y_ref, table_ref, amp_ref, *rest):
    *prior, out_ref, names, names_s, right, acc, sems = rest
    for t in range(GROUPS):
        zero_tail(right, t * FEATS * 8)
    lane = lax.broadcasted_iota(jnp.int32, (8, W), 1)
    mine = (lane >> 4) == lax.broadcasted_iota(jnp.int32, (8, W), 0)
    place = lane & 15
    devices = W
    step, first = len(prior) + 1, len(prior)
    if prior:
        out_ref[pl.ds(0, W, stride=2), :] = prior[0][...]

    def read(g, carry):
        names[pl.ds(g, 1), :] = y_ref[pl.ds(g * ROWS + 24, 1), :].astype(jnp.int32) - 1
        return carry

    lax.fori_loop(0, devices, read, 0, unroll=8)
    move = pltpu.make_async_copy(names, names_s, sems.at[0])
    move.start()
    move.wait()

    def group(i, carry):
        ys, valids = [], []
        for t in range(GROUPS):
            g = i * GROUPS + t
            at = g * ROWS
            y = [y_ref[pl.ds(at + 8 * q, 8), :] for q in range(3)]
            ys.append(y)
            u = [v - 0.5 for v in y]
            scaled = [split3(v * (2.0 * C_FLUID)) for v in u]
            put_rows(right, right_rows(*scaled, norm_of(*u, C_FLUID)), t * FEATS * 8)
        for t in range(GROUPS):
            g = i * GROUPS + t
            valid = jnp.zeros((1, W), jnp.int32)
            for j in range(8):
                name = names_s[g, j]
                valid = jnp.where((lane[0:1] >> 4) == j, name, valid)
                b = jnp.maximum(name, 0)
                kernel = gauss(table_ref[b], take_rows(right, j, t * FEATS * 8).astype(BF))
                res = jnp.dot(amp_ref[b], two_halves(kernel), preferred_element_type=F32)
                spot = 64 * t + 8 * j
                acc[spot : spot + 8, :] = res[0:8] + res[8:16]
            valids.append(valid)
        for t in range(GROUPS):
            g = i * GROUPS + t
            y = ys[t]
            s = [acc[pl.ds(64 * t + q, 8, stride=8), :] for q in range(4)]
            cross = [y[1] * s[2] - y[2] * s[1], y[2] * s[0] - y[0] * s[2],
                     y[0] * s[1] - y[1] * s[0]]
            moment = [y[q] * s[3] for q in range(3)]
            out = jnp.zeros((8, W), F32)
            for q, v in enumerate(s + cross + moment):
                out = jnp.where(place == q, lane_sum(v), out)
            row = jnp.sum(jnp.where(mine, out, 0.0), axis=0, keepdims=True)
            out_ref[pl.ds(step * g + first, 1), :] = jnp.where(valids[t] >= 0, row, 0.0)
        return carry

    lax.fori_loop(0, devices // GROUPS, group, 0)


def fluid(spots, table, amp, *prior):
    vm = pl.BlockSpec(memory_space=pltpu.VMEM)
    return pl.pallas_call(
        fluid_kernel,
        out_shape=jax.ShapeDtypeStruct(((len(prior) + 1) * W, W), F32),
        in_specs=[vm] * (3 + len(prior)),
        out_specs=vm,
        scratch_shapes=[
            pltpu.VMEM((W, W), jnp.int32),
            pltpu.SMEM((W, W), jnp.int32),
            pltpu.VMEM((GROUPS * FEATS * 8, W), F32),
            pltpu.VMEM((GROUPS * 64, W), F32),
            pltpu.SemaphoreType.DMA((1,)),
        ],
        compiler_params=pltpu.CompilerParams(vmem_limit_bytes=12 << 20),
        name="fluid",
    )(spots, table, amp, *prior)


def combine_kernel(dev_ref, rank_ref, off_ref, vel_ref, got_ref, contact_ref, out_ref):
    entries = dev_ref.shape[1]
    clumps = entries // 2
    row = lax.broadcasted_iota(jnp.int32, (W, entries), 0)
    hot = (row == dev_ref[...]).astype(BF)
    rank = rank_ref[...]
    picked = jnp.zeros((16, entries), F32)
    for chunk in range(2):
        spread = jnp.zeros((W, entries), F32)
        for part in split3(jnp.transpose(got_ref[pl.ds(chunk, W, stride=2), :])):
            spread = spread + jnp.dot(part.astype(BF), hot, preferred_element_type=F32)
        spread = jnp.where((row >> 4) + 8 * chunk == rank, spread, 0.0)
        picked = picked + jnp.sum(spread.reshape(8, 16, entries), axis=0)
    touch = jnp.transpose(contact_ref[...])
    total = [touch[q : q + 1, :] for q in range(6)]
    v = [vel_ref[q : q + 1, :] for q in range(3)]
    for k in range(2):
        part = slice(k * clumps, k * clumps + clumps)
        g = [picked[q : q + 1, part] for q in range(10)]
        off = [off_ref[q : q + 1, part] for q in range(3)]
        f = [g[q] - v[q] * g[3] for q in range(3)]
        m = g[7:10]
        for q in range(3):
            a, b = (q + 1) % 3, (q + 2) % 3
            t = g[4 + q] - (m[a] * v[b] - m[b] * v[a]) - (off[a] * f[b] - off[b] * f[a])
            total[q] = total[q] + DRAG * f[q]
            total[3 + q] = total[3 + q] + DRAG * t
    for q in range(6):
        out_ref[q : q + 1, :] = total[q]


def combine(dev, rank, off, vel, got, touch):
    vm = pl.BlockSpec(memory_space=pltpu.VMEM)
    return pl.pallas_call(
        combine_kernel,
        out_shape=jax.ShapeDtypeStruct((6, vel.shape[1]), F32),
        in_specs=[vm] * 6,
        out_specs=vm,
        compiler_params=pltpu.CompilerParams(vmem_limit_bytes=14 << 20),
        name="combine",
    )(dev, rank, off, vel, got, touch)


def extended(cells, sides):
    for axis, dim in sides:
        count = lax.axis_size(axis)
        ends = count - 1
        head = lax.slice_in_dim(cells, 0, 1, axis=dim)
        tail = lax.slice_in_dim(cells, cells.shape[dim] - 1, cells.shape[dim], axis=dim)
        cells = jnp.concatenate(
            [
                lax.ppermute(tail, axis, [(i, (i + 1) % count) for i in range(ends)]),
                cells,
                lax.ppermute(head, axis, [((i + 1) % count, i) for i in range(ends)]),
            ],
            axis=dim,
        )
    return cells


def gate_kernel(array_ref, after_ref, out_ref):
    del array_ref, after_ref, out_ref


def gated(array, after):
    hbm = pl.BlockSpec(memory_space=pltpu.HBM)
    return pl.pallas_call(
        gate_kernel,
        out_shape=jax.ShapeDtypeStruct(array.shape, array.dtype),
        in_specs=[hbm, pl.BlockSpec(memory_space=pl.ANY)],
        out_specs=hbm,
        input_output_aliases={0: 0},
        name="gate",
    )(array, after)


def swap_all(array):
    return lax.all_to_all(array, AXES, split_axis=0, concat_axis=0, tiled=True)


def body(
    fluid_pos,
    fluid_vel,
    fluid_mass,
    fluid_count,
    clump_center,
    clump_vel,
    clump_arm,
    margin_device,
    margin_block,
    margin_offset,
    contact_partner,
):
    rows_x, rows_y, width = fluid_mass.shape
    blocks = rows_x * rows_y
    clumps = clump_arm.shape[0]
    entries = 2 * clumps
    devices = lax.axis_size(AXES)
    arms = jnp.transpose(clump_arm, (1, 0, 2))
    world = arms + clump_center.T[:, :, None]
    following = lax.ppermute(world, AXES, [(i, (i + devices - 1) % devices) for i in range(devices)])
    lanes = jnp.arange(width, dtype=jnp.int32)
    live = jnp.where(lanes[None, None, :] < fluid_count[..., None], fluid_mass, 0.0)
    planes = jnp.concatenate([jnp.moveaxis(fluid_pos, 2, 0), live[None]], axis=0)
    tall = extended(planes, (("stream", 1),))
    dev = margin_device.T.reshape(1, entries)
    blk = margin_block.T.reshape(1, entries)
    off = jnp.transpose(margin_offset, (2, 1, 0)).reshape(3, entries)
    vel = clump_vel.T
    dev, tall = lax.optimization_barrier((dev, tall))
    ext = extended(tall, (("span", 2),))
    first, second, rank = prep(dev, blk, off, arms)
    first, second, ext, following = lax.optimization_barrier((first, second, ext, following))
    got_first = swap_all(first.reshape(devices, 1, ROWS * width))
    ext = ext.reshape(4, (rows_x + 2) * (rows_y + 2), width)
    ext = jnp.pad(ext, ((0, 0), (0, 4), (0, 0)))
    own = planes.reshape(4, blocks, width)
    speed = jnp.moveaxis(fluid_vel, 2, 0).reshape(3, blocks, width)
    dens, table, amp = density(ext, own, fluid_mass.reshape(blocks, width), speed)
    touch, done = contact(contact_partner.reshape(1, clumps), arms, world, following, dens)
    second = gated(second, done)
    got_second = swap_all(second.reshape(devices, 1, ROWS * width))
    one = fluid(got_first.reshape(devices * ROWS, width), table, amp)
    both = fluid(got_second.reshape(devices * ROWS, width), table, amp, one)
    back = swap_all(both.reshape(devices, 1, 2 * width)).reshape(2 * devices, width)
    loads = combine(dev, rank, off, vel, back, touch)
    return (dens.reshape(rows_x, rows_y, width), loads)


def solution(mesh):
    in_specs = (
        P("stream", "span", None, None),
        P("stream", "span", None, None),
        P("stream", "span", None),
        P("stream", "span"),
        P(("stream", "span"), None),
        P(("stream", "span"), None),
        P(("stream", "span"), None, None),
        P(("stream", "span"), None),
        P(("stream", "span"), None),
        P(("stream", "span"), None, None),
        P(("stream", "span")),
    )
    out_specs = (P("stream", "span", None), P(None, ("stream", "span")))
    return jax.shard_map(body, mesh=mesh, in_specs=in_specs, out_specs=out_specs, check_vma=False)
```

```python
import functools
import math

import jax
import jax.numpy as jnp
from jax import lax
from jax.experimental import pallas as pl
from jax.experimental.pallas import tpu as pltpu
from jax.sharding import PartitionSpec as P

H_SQ = 0.25
SIG_SQ = 0.5
DENS = 0.03125
DRAG = 0.002
STIFF = 0.005
LOG2E = math.log2(math.e)
C_FLUID = LOG2E / H_SQ
C_CONTACT = LOG2E / SIG_SQ
AXES = ("stream", "span")
W = 128
FEATS = 32
ROWS = 49
UNROLL = 4
GROUPS = 16
DEAD = -30000.0
BF = jnp.bfloat16
F32 = jnp.float32


def split3(v):
    hi = v.astype(BF).astype(F32)
    rest = v - hi
    mid = rest.astype(BF).astype(F32)
    return hi, mid, rest - mid


def norm_of(x, y, z, coef):
    return (x * x + y * y + z * z) * (-coef)


def left_rows(xs, ys, zs, norm):
    h, m, low = ([c[i] for c in (xs, ys, zs)] for i in range(3))
    one = jnp.ones_like(h[0])
    return h + h + h + m + m + low + list(split3(norm)) + [one, one, one]


def right_rows(xs, ys, zs, norm):
    h, m, low = ([c[i] for c in (xs, ys, zs)] for i in range(3))
    one = jnp.ones_like(h[0])
    return h + m + low + h + m + h + [one, one, one] + list(split3(norm))


def put_rows(ref, rows, base=0):
    for i, row in enumerate(rows):
        ref[base + 8 * i : base + 8 * i + 8, :] = row


def zero_tail(ref, base=0):
    zero = jnp.zeros((8, W), F32)
    for i in range(24, FEATS):
        ref[base + 8 * i : base + 8 * i + 8, :] = zero


def take_rows(ref, j, base=0):
    return ref[pl.ds(base + j, FEATS, stride=8), :]


def gauss(left, right):
    return jnp.exp2(jnp.dot(left, right, preferred_element_type=F32))


def two_halves(kernel):
    hi = kernel.astype(BF)
    lo = (kernel - hi.astype(F32)).astype(BF)
    return jnp.concatenate([hi, lo], axis=0)


def lane_sum(v):
    return jnp.sum(v, axis=1, keepdims=True)


def prep_kernel(dev_ref, blk_ref, dev_s, off_s, arm_ref, send_ref, rank_ref, buf, rank_s, sems):
    entries = dev_ref.shape[1]
    parts = entries // W
    dev = dev_ref[...]
    row = lax.broadcasted_iota(jnp.int32, (W, entries), 0)
    hot = (row == dev).astype(F32)
    hot_b = hot.astype(BF)
    up = lax.broadcasted_iota(jnp.int32, (W, 2 * W), 0)
    lane = lax.broadcasted_iota(jnp.int32, (W, 2 * W), 1)
    tri = jnp.where(lane >= W, 1.0, jnp.where(up < lane, 1.0, 0.0)).astype(BF)
    carry = jnp.zeros((W, W), F32)
    ranks = []
    for part in range(parts):
        piece = slice(part * W, part * W + W)
        both = jnp.dot(hot_b[:, piece], tri, preferred_element_type=F32)
        ranks.append(jnp.sum(hot[:, piece] * (both[:, :W] + carry), axis=0, keepdims=True))
        carry = carry + both[:, W:]
    rank = jnp.concatenate(ranks, axis=1).astype(jnp.int32)
    rank_ref[...] = rank
    move = pltpu.make_async_copy(rank_ref, rank_s, sems.at[0])
    move.start()
    named = jnp.where(row == rank, blk_ref[...] + 1, 0).astype(F32).astype(BF)
    ids = lax.dot_general(hot_b, named, (((1,), (1,)), ((), ())), preferred_element_type=F32)
    for d in range(W):
        buf[d * ROWS + 48 : d * ROWS + 49, :] = ids[d : d + 1, :]
    move.wait()

    clumps = entries // 2

    def step(i, carry):
        for k in range(2):
            for j in range(8):
                c = i * 8 + j
                e = k * clumps + c
                base = dev_s[0, e] * ROWS + rank_s[0, e]
                for q in range(3):
                    buf[pl.ds(base + 16 * q, 1), :] = (
                        arm_ref[q, pl.ds(c, 1), :] + off_s[q, e]
                    )
        return carry

    lax.fori_loop(0, clumps // 8, step, 0)
    out = pltpu.make_async_copy(buf, send_ref, sems.at[0])
    out.start()
    out.wait()


def prep(dev, blk, off, arms):
    entries = dev.shape[1]
    vm = pl.BlockSpec(memory_space=pltpu.VMEM)
    sm = pl.BlockSpec(memory_space=pltpu.SMEM)
    hbm = pl.BlockSpec(memory_space=pltpu.HBM)
    return pl.pallas_call(
        prep_kernel,
        out_shape=(
            jax.ShapeDtypeStruct((W * ROWS, W), F32),
            jax.ShapeDtypeStruct((1, entries), jnp.int32),
        ),
        in_specs=[vm, vm, sm, sm, vm],
        out_specs=(hbm, vm),
        scratch_shapes=[
            pltpu.VMEM((W * ROWS, W), F32),
            pltpu.SMEM((1, entries), jnp.int32),
            pltpu.SemaphoreType.DMA((1,)),
        ],
        compiler_params=pltpu.CompilerParams(vmem_limit_bytes=40 << 20),
        name="prep",
    )(dev, blk, dev, off, arms)


def density_kernel(ext_ref, own_ref, mass_ref, vel_ref, dens_ref, table_ref, amp_ref,
                   feat, right, sums, left, wide):
    rows_y = 8
    zero_tail(feat)
    for s in range(9):
        zero_tail(right, s * FEATS * 8)

    def coords(ref, at):
        return [ref[q, pl.ds(at, 8), :] - 0.5 for q in range(3)]

    def ext_group(g, carry):
        at = pl.multiple_of(g * 8, 8)
        x, y, z = coords(ext_ref, at)
        m = ext_ref[3, pl.ds(at, 8), :]
        logm = jnp.where(m > 0.0, jnp.log2(jnp.where(m > 0.0, m, 1.0)), DEAD)
        norm = norm_of(x, y, z, C_FLUID) + logm
        put_rows(feat, left_rows(split3(x), split3(y), split3(z), norm))
        for j in range(8):
            left[at + j] = jnp.transpose(take_rows(feat, j)).astype(BF)
        return carry

    lax.fori_loop(0, ext_ref.shape[1] // 8, ext_group, 0)

    def own_row(a, carry):
        at = pl.multiple_of(a * 8, 8)
        x, y, z = coords(own_ref, at)
        xs = [x + 1.0, x, x - 1.0]
        ys = [y + 1.0, y, y - 1.0]
        scale = 2.0 * C_FLUID
        xsplit = [split3(v * scale) for v in xs]
        ysplit = [split3(v * scale) for v in ys]
        zsplit = split3(z * scale)
        for ix in range(3):
            for iy in range(3):
                norm = norm_of(xs[ix], ys[iy], z, C_FLUID)
                put_rows(right, right_rows(xsplit[ix], ysplit[iy], zsplit, norm),
                         (ix * 3 + iy) * FEATS * 8)

        def block(b, inner):
            total = jnp.zeros((8, W), F32)
            for ix in range(3):
                for iy in range(3):
                    rhs = take_rows(right, b, (ix * 3 + iy) * FEATS * 8).astype(BF)
                    lhs = left[(a + ix) * 10 + b + iy]
                    total = total + jnp.sum(gauss(lhs, rhs).reshape(16, 8, W), axis=0)
            sums[pl.ds(b, 1), :] = jnp.sum(total, axis=0, keepdims=True)
            return inner

        lax.fori_loop(0, rows_y, block, 0, unroll=4)
        density = DENS * (mass_ref[pl.ds(at, 8), :] + sums[...])
        dens_ref[pl.ds(at, 8), :] = density
        weight = own_ref[3, pl.ds(at, 8), :] / density
        parts = [vel_ref[q, pl.ds(at, 8), :] * weight for q in range(3)] + [weight]
        zero = jnp.zeros((8, W), F32)
        for q, v in enumerate(parts):
            hi = v.astype(BF).astype(F32)
            wide[8 * q : 8 * q + 8, :] = hi
            wide[8 * (q + 8) : 8 * (q + 8) + 8, :] = v - hi
        for q in (4, 5, 6, 7, 12, 13, 14, 15):
            wide[8 * q : 8 * q + 8, :] = zero
        norm = norm_of(x, y, z, C_FLUID)
        put_rows(feat, left_rows(split3(x), split3(y), split3(z), norm))
        upper = lax.broadcasted_iota(jnp.int32, (16, W), 0) < 8
        for j in range(8):
            table_ref[at + j] = jnp.transpose(take_rows(feat, j)).astype(BF)
            a16 = wide[pl.ds(j, 16, stride=8), :]
            amp_ref[at + j, :, 0:W] = a16.astype(BF)
            amp_ref[at + j, :, W : 2 * W] = jnp.where(upper, a16, 0.0).astype(BF)
        return carry

    lax.fori_loop(0, 8, own_row, 0)


def density(ext, own, mass, vel):
    blocks = mass.shape[0]
    vm = pl.BlockSpec(memory_space=pltpu.VMEM)
    return pl.pallas_call(
        density_kernel,
        out_shape=(
            jax.ShapeDtypeStruct((blocks, W), F32),
            jax.ShapeDtypeStruct((blocks, W, FEATS), BF),
            jax.ShapeDtypeStruct((blocks, 16, 2 * W), BF),
        ),
        in_specs=[vm] * 4,
        out_specs=(vm, vm, vm),
        scratch_shapes=[
            pltpu.VMEM((FEATS * 8, W), F32),
            pltpu.VMEM((9 * FEATS * 8, W), F32),
            pltpu.VMEM((8, W), F32),
            pltpu.VMEM((ext.shape[1], W, FEATS), BF),
            pltpu.VMEM((W, W), F32),
        ],
        compiler_params=pltpu.CompilerParams(vmem_limit_bytes=14 << 20),
        name="density",
    )(ext, own, mass, vel)


def columns_to_lanes(cols):
    lane = lax.broadcasted_iota(jnp.int32, (8, W), 1)
    out = jnp.zeros((8, W), F32)
    for q, col in enumerate(cols):
        out = jnp.where(lane == q, col, out)
    return out


def contact_kernel(partner_s, arm_ref, world_ref, next_ref, after_ref, out_ref, done_ref, cand, gat, feat, right, lead, acc):
    clumps = arm_ref.shape[1]
    done_ref[...] = jnp.zeros_like(done_ref)
    cand[:, 0:clumps, :] = world_ref[...]
    cand[:, clumps : 2 * clumps, :] = next_ref[...]
    zero = jnp.zeros((8, W), F32)
    for t in range(UNROLL):
        zero_tail(feat, t * FEATS * 8)
        zero_tail(right, t * FEATS * 8)
        for q in (4, 5, 6, 7, 12, 13, 14, 15):
            lead[t * W + 8 * q : t * W + 8 * q + 8, :] = zero
    upper = lax.broadcasted_iota(jnp.int32, (16, W), 0) < 8

    def group(i, carry):
        zas, ats = [], []
        for t in range(UNROLL):
            at = pl.multiple_of((i * UNROLL + t) * 8, 8)
            ats.append(at)
            for j in range(8):
                p = partner_s[0, at + j]
                for q in range(3):
                    spot = 24 * t + 8 * q + j
                    gat[spot : spot + 1, :] = cand[q, pl.ds(p, 1), :]
            za = [world_ref[q, pl.ds(at, 8), :] - 0.5 for q in range(3)]
            zas.append(za)
            scaled = [split3(v * (2.0 * C_CONTACT)) for v in za]
            put_rows(right, right_rows(*scaled, norm_of(*za, C_CONTACT)), t * FEATS * 8)
        for t in range(UNROLL):
            zb = [gat[24 * t + 8 * q : 24 * t + 8 * q + 8, :] - 0.5 for q in range(3)]
            parts = [split3(v) for v in zb]
            put_rows(feat, left_rows(*parts, norm_of(*zb, C_CONTACT)), t * FEATS * 8)
            for q, v in enumerate(zb + [jnp.ones((8, W), F32)]):
                hi = v.astype(BF).astype(F32)
                spot = t * W + 8 * q
                lead[spot : spot + 8, :] = hi
                lead[spot + 64 : spot + 72, :] = v - hi
        for t in range(UNROLL):
            for j in range(8):
                lhs = jnp.transpose(take_rows(feat, j, t * FEATS * 8)).astype(BF)
                kernel = gauss(lhs, take_rows(right, j, t * FEATS * 8).astype(BF))
                l16 = lead[pl.ds(t * W + j, 16, stride=8), :]
                both = jnp.concatenate([l16, jnp.where(upper, l16, 0.0)], axis=1).astype(BF)
                res = jnp.dot(both, two_halves(kernel), preferred_element_type=F32)
                spot = 64 * t + 8 * j
                acc[spot : spot + 8, :] = res[0:8] + res[8:16]
        for t in range(UNROLL):
            at, za = ats[t], zas[t]
            s = [acc[pl.ds(64 * t + q, 8, stride=8), :] for q in range(4)]
            f = [STIFF * (za[q] * s[3] - s[q]) for q in range(3)]
            arm = [arm_ref[q, pl.ds(at, 8), :] for q in range(3)]
            tq = [arm[1] * f[2] - arm[2] * f[1], arm[2] * f[0] - arm[0] * f[2],
                  arm[0] * f[1] - arm[1] * f[0]]
            out_ref[pl.ds(at, 8), :] = columns_to_lanes([lane_sum(v) for v in f + tq])
        return carry

    lax.fori_loop(0, clumps // (8 * UNROLL), group, 0)


def contact(partner, arms, world, following, after):
    clumps = arms.shape[1]
    vm = pl.BlockSpec(memory_space=pltpu.VMEM)
    sm = pl.BlockSpec(memory_space=pltpu.SMEM)
    return pl.pallas_call(
        contact_kernel,
        out_shape=(jax.ShapeDtypeStruct((clumps, W), F32), jax.ShapeDtypeStruct((8, W), F32)),
        in_specs=[sm, vm, vm, vm, pl.BlockSpec(memory_space=pl.ANY)],
        out_specs=(vm, vm),
        scratch_shapes=[
            pltpu.VMEM((3, 2 * clumps, W), F32),
            pltpu.VMEM((UNROLL * 24, W), F32),
            pltpu.VMEM((UNROLL * FEATS * 8, W), F32),
            pltpu.VMEM((UNROLL * FEATS * 8, W), F32),
            pltpu.VMEM((UNROLL * W, W), F32),
            pltpu.VMEM((UNROLL * 64, W), F32),
        ],
        compiler_params=pltpu.CompilerParams(vmem_limit_bytes=10 << 20),
        name="contact",
    )(partner, arms, world, following, after)


def fluid_kernel(y_ref, table_hbm, amp_hbm, after_ref, out_ref, names, names_s, right, acc,
                 table_ref, amp_ref, sems):
    load = [
        pltpu.make_async_copy(table_hbm, table_ref, sems.at[1]),
        pltpu.make_async_copy(amp_hbm, amp_ref, sems.at[2]),
    ]
    for copy in load:
        copy.start()
    for t in range(GROUPS):
        zero_tail(right, t * FEATS * 8)
    lane = lax.broadcasted_iota(jnp.int32, (8, W), 1)
    mine = (lane >> 4) == lax.broadcasted_iota(jnp.int32, (8, W), 0)
    place = lane & 15
    devices = out_ref.shape[0] // 2

    def read(g, carry):
        names[pl.ds(g, 1), :] = y_ref[pl.ds(g * ROWS + 48, 1), :].astype(jnp.int32) - 1
        return carry

    lax.fori_loop(0, devices, read, 0, unroll=8)
    move = pltpu.make_async_copy(names, names_s, sems.at[0])
    move.start()
    move.wait()
    for copy in load:
        copy.wait()

    def group(i, carry):
        ys, valids = [], []
        for t in range(GROUPS):
            g = i * (GROUPS // 2) + t // 2
            at = g * ROWS + (t % 2) * 8
            y = [y_ref[pl.ds(at + 16 * q, 8), :] for q in range(3)]
            ys.append(y)
            u = [v - 0.5 for v in y]
            scaled = [split3(v * (2.0 * C_FLUID)) for v in u]
            put_rows(right, right_rows(*scaled, norm_of(*u, C_FLUID)), t * FEATS * 8)
        for t in range(GROUPS):
            g = i * (GROUPS // 2) + t // 2
            valid = jnp.zeros((1, W), jnp.int32)
            for j in range(8):
                name = names_s[g, (t % 2) * 8 + j]
                valid = jnp.where((lane[0:1] >> 4) == j, name, valid)
                b = jnp.maximum(name, 0)
                kernel = gauss(table_ref[b], take_rows(right, j, t * FEATS * 8).astype(BF))
                res = jnp.dot(amp_ref[b], two_halves(kernel), preferred_element_type=F32)
                spot = 64 * t + 8 * j
                acc[spot : spot + 8, :] = res[0:8] + res[8:16]
            valids.append(valid)
        for t in range(GROUPS):
            g = i * (GROUPS // 2) + t // 2
            y = ys[t]
            s = [acc[pl.ds(64 * t + q, 8, stride=8), :] for q in range(4)]
            cross = [y[1] * s[2] - y[2] * s[1], y[2] * s[0] - y[0] * s[2],
                     y[0] * s[1] - y[1] * s[0]]
            moment = [y[q] * s[3] for q in range(3)]
            out = jnp.zeros((8, W), F32)
            for q, v in enumerate(s + cross + moment):
                out = jnp.where(place == q, lane_sum(v), out)
            row = jnp.sum(jnp.where(mine, out, 0.0), axis=0, keepdims=True)
            out_ref[pl.ds(2 * g + t % 2, 1), :] = jnp.where(valids[t] >= 0, row, 0.0)
        return carry

    lax.fori_loop(0, devices // (GROUPS // 2), group, 0)


def fluid(spots, table, amp, after):
    vm = pl.BlockSpec(memory_space=pltpu.VMEM)
    hbm = pl.BlockSpec(memory_space=pltpu.HBM)
    return pl.pallas_call(
        fluid_kernel,
        out_shape=jax.ShapeDtypeStruct((2 * W, W), F32),
        in_specs=[vm, hbm, hbm, hbm],
        out_specs=vm,
        scratch_shapes=[
            pltpu.VMEM((W, W), jnp.int32),
            pltpu.SMEM((W, W), jnp.int32),
            pltpu.VMEM((GROUPS * FEATS * 8, W), F32),
            pltpu.VMEM((GROUPS * 64, W), F32),
            pltpu.VMEM(table.shape, BF),
            pltpu.VMEM(amp.shape, BF),
            pltpu.SemaphoreType.DMA((3,)),
        ],
        compiler_params=pltpu.CompilerParams(vmem_limit_bytes=18 << 20),
        name="fluid",
    )(spots, table, amp, after)


def combine_kernel(dev_ref, rank_ref, off_ref, vel_ref, got_ref, contact_ref, out_ref):
    entries = dev_ref.shape[1]
    clumps = entries // 2
    row = lax.broadcasted_iota(jnp.int32, (W, entries), 0)
    hot = (row == dev_ref[...]).astype(BF)
    rank = rank_ref[...]
    picked = jnp.zeros((16, entries), F32)
    for chunk in range(2):
        spread = jnp.zeros((W, entries), F32)
        for part in split3(jnp.transpose(got_ref[pl.ds(chunk, W, stride=2), :])):
            spread = spread + jnp.dot(part.astype(BF), hot, preferred_element_type=F32)
        spread = jnp.where((row >> 4) + 8 * chunk == rank, spread, 0.0)
        picked = picked + jnp.sum(spread.reshape(8, 16, entries), axis=0)
    touch = jnp.transpose(contact_ref[...])
    total = [touch[q : q + 1, :] for q in range(6)]
    v = [vel_ref[q : q + 1, :] for q in range(3)]
    for k in range(2):
        part = slice(k * clumps, k * clumps + clumps)
        g = [picked[q : q + 1, part] for q in range(10)]
        off = [off_ref[q : q + 1, part] for q in range(3)]
        f = [g[q] - v[q] * g[3] for q in range(3)]
        m = g[7:10]
        for q in range(3):
            a, b = (q + 1) % 3, (q + 2) % 3
            t = g[4 + q] - (m[a] * v[b] - m[b] * v[a]) - (off[a] * f[b] - off[b] * f[a])
            total[q] = total[q] + DRAG * f[q]
            total[3 + q] = total[3 + q] + DRAG * t
    for q in range(6):
        out_ref[q : q + 1, :] = total[q]


def combine(dev, rank, off, vel, got, touch):
    vm = pl.BlockSpec(memory_space=pltpu.VMEM)
    return pl.pallas_call(
        combine_kernel,
        out_shape=jax.ShapeDtypeStruct((6, vel.shape[1]), F32),
        in_specs=[vm] * 6,
        out_specs=vm,
        compiler_params=pltpu.CompilerParams(vmem_limit_bytes=14 << 20),
        name="combine",
    )(dev, rank, off, vel, got, touch)


def extended(cells, sides):
    for axis, dim in sides:
        count = lax.axis_size(axis)
        ends = count - 1
        head = lax.slice_in_dim(cells, 0, 1, axis=dim)
        tail = lax.slice_in_dim(cells, cells.shape[dim] - 1, cells.shape[dim], axis=dim)
        cells = jnp.concatenate(
            [
                lax.ppermute(tail, axis, [(i, (i + 1) % count) for i in range(ends)]),
                cells,
                lax.ppermute(head, axis, [((i + 1) % count, i) for i in range(ends)]),
            ],
            axis=dim,
        )
    return cells


def swap_all(array):
    return lax.all_to_all(array, AXES, split_axis=0, concat_axis=0, tiled=True)


def body(
    fluid_pos,
    fluid_vel,
    fluid_mass,
    fluid_count,
    clump_center,
    clump_vel,
    clump_arm,
    margin_device,
    margin_block,
    margin_offset,
    contact_partner,
):
    rows_x, rows_y, width = fluid_mass.shape
    blocks = rows_x * rows_y
    clumps = clump_arm.shape[0]
    entries = 2 * clumps
    devices = lax.axis_size(AXES)
    arms = jnp.transpose(clump_arm, (1, 0, 2))
    world = arms + clump_center.T[:, :, None]
    following = lax.ppermute(world, AXES, [(i, (i + devices - 1) % devices) for i in range(devices)])
    lanes = jnp.arange(width, dtype=jnp.int32)
    live = jnp.where(lanes[None, None, :] < fluid_count[..., None], fluid_mass, 0.0)
    planes = jnp.concatenate([jnp.moveaxis(fluid_pos, 2, 0), live[None]], axis=0)
    tall = extended(planes, (("stream", 1),))
    dev = margin_device.T.reshape(1, entries)
    blk = margin_block.T.reshape(1, entries)
    off = jnp.transpose(margin_offset, (2, 1, 0)).reshape(3, entries)
    vel = clump_vel.T
    dev, tall = lax.optimization_barrier((dev, tall))
    ext = extended(tall, (("span", 2),))
    send, rank = prep(dev, blk, off, arms)
    send, ext, following = lax.optimization_barrier((send, ext, following))
    got = swap_all(send.reshape(devices, 1, ROWS * width))
    ext = ext.reshape(4, (rows_x + 2) * (rows_y + 2), width)
    ext = jnp.pad(ext, ((0, 0), (0, 4), (0, 0)))
    own = planes.reshape(4, blocks, width)
    speed = jnp.moveaxis(fluid_vel, 2, 0).reshape(3, blocks, width)
    dens, table, amp = density(ext, own, fluid_mass.reshape(blocks, width), speed)
    touch, done = contact(contact_partner.reshape(1, clumps), arms, world, following, dens)
    sums = fluid(got.reshape(devices * ROWS, width), table, amp, done)
    back = swap_all(sums.reshape(devices, 1, 2 * width)).reshape(2 * devices, width)
    loads = combine(dev, rank, off, vel, back, touch)
    return (dens.reshape(rows_x, rows_y, width), loads)


def solution(mesh):
    in_specs = (
        P("stream", "span", None, None),
        P("stream", "span", None, None),
        P("stream", "span", None),
        P("stream", "span"),
        P(("stream", "span"), None),
        P(("stream", "span"), None),
        P(("stream", "span"), None, None),
        P(("stream", "span"), None),
        P(("stream", "span"), None),
        P(("stream", "span"), None, None),
        P(("stream", "span")),
    )
    out_specs = (P("stream", "span", None), P(None, ("stream", "span")))
    return jax.shard_map(body, mesh=mesh, in_specs=in_specs, out_specs=out_specs, check_vma=False)
```

```python
import functools
import math

import jax
import jax.numpy as jnp
from jax import lax
from jax.experimental import pallas as pl
from jax.experimental.pallas import tpu as pltpu
from jax.sharding import PartitionSpec as P

H_SQ = 0.25
SIG_SQ = 0.5
DENS = 0.03125
DRAG = 0.002
STIFF = 0.005
LOG2E = math.log2(math.e)
C_FLUID = LOG2E / H_SQ
C_CONTACT = LOG2E / SIG_SQ
AXES = ("stream", "span")
W = 128
FEATS = 32
ROWS = 49
UNROLL = 4
GROUPS = 16
DEAD = -30000.0
BF = jnp.bfloat16
F32 = jnp.float32


def split3(v):
    hi = v.astype(BF).astype(F32)
    rest = v - hi
    mid = rest.astype(BF).astype(F32)
    return hi, mid, rest - mid


def norm_of(x, y, z, coef):
    return (x * x + y * y + z * z) * (-coef)


def left_rows(xs, ys, zs, norm):
    h, m, low = ([c[i] for c in (xs, ys, zs)] for i in range(3))
    one = jnp.ones_like(h[0])
    return h + h + h + m + m + low + list(split3(norm)) + [one, one, one]


def right_rows(xs, ys, zs, norm):
    h, m, low = ([c[i] for c in (xs, ys, zs)] for i in range(3))
    one = jnp.ones_like(h[0])
    return h + m + low + h + m + h + [one, one, one] + list(split3(norm))


def put_rows(ref, rows, base=0):
    for i, row in enumerate(rows):
        ref[base + 8 * i : base + 8 * i + 8, :] = row


def zero_tail(ref, base=0):
    zero = jnp.zeros((8, W), F32)
    for i in range(24, FEATS):
        ref[base + 8 * i : base + 8 * i + 8, :] = zero


def take_rows(ref, j, base=0):
    return ref[pl.ds(base + j, FEATS, stride=8), :]


def gauss(left, right):
    return jnp.exp2(jnp.dot(left, right, preferred_element_type=F32))


def two_halves(kernel):
    hi = kernel.astype(BF)
    lo = (kernel - hi.astype(F32)).astype(BF)
    return jnp.concatenate([hi, lo], axis=0)


def lane_sum(v):
    return jnp.sum(v, axis=1, keepdims=True)


def prep_kernel(dev_ref, blk_ref, dev_s, off_s, arm_ref, send_ref, rank_ref, buf, rank_s, sems):
    entries = dev_ref.shape[1]
    parts = entries // W
    dev = dev_ref[...]
    row = lax.broadcasted_iota(jnp.int32, (W, entries), 0)
    hot = (row == dev).astype(F32)
    hot_b = hot.astype(BF)
    up = lax.broadcasted_iota(jnp.int32, (W, 2 * W), 0)
    lane = lax.broadcasted_iota(jnp.int32, (W, 2 * W), 1)
    tri = jnp.where(lane >= W, 1.0, jnp.where(up < lane, 1.0, 0.0)).astype(BF)
    carry = jnp.zeros((W, W), F32)
    ranks = []
    for part in range(parts):
        piece = slice(part * W, part * W + W)
        both = jnp.dot(hot_b[:, piece], tri, preferred_element_type=F32)
        ranks.append(jnp.sum(hot[:, piece] * (both[:, :W] + carry), axis=0, keepdims=True))
        carry = carry + both[:, W:]
    rank = jnp.concatenate(ranks, axis=1).astype(jnp.int32)
    rank_ref[...] = rank
    move = pltpu.make_async_copy(rank_ref, rank_s, sems.at[0])
    move.start()
    named = jnp.where(row == rank, blk_ref[...] + 1, 0).astype(F32).astype(BF)
    ids = lax.dot_general(hot_b, named, (((1,), (1,)), ((), ())), preferred_element_type=F32)
    for d in range(W):
        buf[d * ROWS + 48 : d * ROWS + 49, :] = ids[d : d + 1, :]
    move.wait()

    clumps = entries // 2

    def step(i, carry):
        for k in range(2):
            for j in range(8):
                c = i * 8 + j
                e = k * clumps + c
                base = dev_s[0, e] * ROWS + rank_s[0, e]
                for q in range(3):
                    buf[pl.ds(base + 16 * q, 1), :] = (
                        arm_ref[q, pl.ds(c, 1), :] + off_s[q, e]
                    )
        return carry

    lax.fori_loop(0, clumps // 8, step, 0)
    out = pltpu.make_async_copy(buf, send_ref, sems.at[0])
    out.start()
    out.wait()


def prep(dev, blk, off, arms):
    entries = dev.shape[1]
    vm = pl.BlockSpec(memory_space=pltpu.VMEM)
    sm = pl.BlockSpec(memory_space=pltpu.SMEM)
    hbm = pl.BlockSpec(memory_space=pltpu.HBM)
    return pl.pallas_call(
        prep_kernel,
        out_shape=(
            jax.ShapeDtypeStruct((W * ROWS, W), F32),
            jax.ShapeDtypeStruct((1, entries), jnp.int32),
        ),
        in_specs=[vm, vm, sm, sm, vm],
        out_specs=(hbm, vm),
        scratch_shapes=[
            pltpu.VMEM((W * ROWS, W), F32),
            pltpu.SMEM((1, entries), jnp.int32),
            pltpu.SemaphoreType.DMA((1,)),
        ],
        compiler_params=pltpu.CompilerParams(vmem_limit_bytes=40 << 20),
        name="prep",
    )(dev, blk, dev, off, arms)


def density_kernel(ext_ref, own_ref, mass_ref, vel_ref, after_ref, dens_ref, table_ref, amp_ref,
                   feat, right, sums, left, wide):
    rows_y = 8
    zero_tail(feat)
    for s in range(9):
        zero_tail(right, s * FEATS * 8)

    def coords(ref, at):
        return [ref[q, pl.ds(at, 8), :] - 0.5 for q in range(3)]

    def ext_group(g, carry):
        at = pl.multiple_of(g * 8, 8)
        x, y, z = coords(ext_ref, at)
        m = ext_ref[3, pl.ds(at, 8), :]
        logm = jnp.where(m > 0.0, jnp.log2(jnp.where(m > 0.0, m, 1.0)), DEAD)
        norm = norm_of(x, y, z, C_FLUID) + logm
        put_rows(feat, left_rows(split3(x), split3(y), split3(z), norm))
        for j in range(8):
            left[at + j] = jnp.transpose(take_rows(feat, j)).astype(BF)
        return carry

    lax.fori_loop(0, ext_ref.shape[1] // 8, ext_group, 0)

    def own_row(a, carry):
        at = pl.multiple_of(a * 8, 8)
        x, y, z = coords(own_ref, at)
        xs = [x + 1.0, x, x - 1.0]
        ys = [y + 1.0, y, y - 1.0]
        scale = 2.0 * C_FLUID
        xsplit = [split3(v * scale) for v in xs]
        ysplit = [split3(v * scale) for v in ys]
        zsplit = split3(z * scale)
        for ix in range(3):
            for iy in range(3):
                norm = norm_of(xs[ix], ys[iy], z, C_FLUID)
                put_rows(right, right_rows(xsplit[ix], ysplit[iy], zsplit, norm),
                         (ix * 3 + iy) * FEATS * 8)

        def block(b, inner):
            total = jnp.zeros((8, W), F32)
            for ix in range(3):
                for iy in range(3):
                    rhs = take_rows(right, b, (ix * 3 + iy) * FEATS * 8).astype(BF)
                    lhs = left[(a + ix) * 10 + b + iy]
                    total = total + jnp.sum(gauss(lhs, rhs).reshape(16, 8, W), axis=0)
            sums[pl.ds(b, 1), :] = jnp.sum(total, axis=0, keepdims=True)
            return inner

        lax.fori_loop(0, rows_y, block, 0, unroll=4)
        density = DENS * (mass_ref[pl.ds(at, 8), :] + sums[...])
        dens_ref[pl.ds(at, 8), :] = density
        weight = own_ref[3, pl.ds(at, 8), :] / density
        parts = [vel_ref[q, pl.ds(at, 8), :] * weight for q in range(3)] + [weight]
        zero = jnp.zeros((8, W), F32)
        for q, v in enumerate(parts):
            hi = v.astype(BF).astype(F32)
            wide[8 * q : 8 * q + 8, :] = hi
            wide[8 * (q + 8) : 8 * (q + 8) + 8, :] = v - hi
        for q in (4, 5, 6, 7, 12, 13, 14, 15):
            wide[8 * q : 8 * q + 8, :] = zero
        norm = norm_of(x, y, z, C_FLUID)
        put_rows(feat, left_rows(split3(x), split3(y), split3(z), norm))
        upper = lax.broadcasted_iota(jnp.int32, (16, W), 0) < 8
        for j in range(8):
            table_ref[at + j] = jnp.transpose(take_rows(feat, j)).astype(BF)
            a16 = wide[pl.ds(j, 16, stride=8), :]
            amp_ref[at + j, :, 0:W] = a16.astype(BF)
            amp_ref[at + j, :, W : 2 * W] = jnp.where(upper, a16, 0.0).astype(BF)
        return carry

    lax.fori_loop(0, 8, own_row, 0)


def density(ext, own, mass, vel, after):
    blocks = mass.shape[0]
    vm = pl.BlockSpec(memory_space=pltpu.VMEM)
    return pl.pallas_call(
        density_kernel,
        out_shape=(
            jax.ShapeDtypeStruct((blocks, W), F32),
            jax.ShapeDtypeStruct((blocks, W, FEATS), BF),
            jax.ShapeDtypeStruct((blocks, 16, 2 * W), BF),
        ),
        in_specs=[vm] * 5,
        out_specs=(vm, vm, vm),
        scratch_shapes=[
            pltpu.VMEM((FEATS * 8, W), F32),
            pltpu.VMEM((9 * FEATS * 8, W), F32),
            pltpu.VMEM((8, W), F32),
            pltpu.VMEM((ext.shape[1], W, FEATS), BF),
            pltpu.VMEM((W, W), F32),
        ],
        compiler_params=pltpu.CompilerParams(vmem_limit_bytes=14 << 20),
        name="density",
    )(ext, own, mass, vel, after)


def columns_to_lanes(cols):
    lane = lax.broadcasted_iota(jnp.int32, (8, W), 1)
    out = jnp.zeros((8, W), F32)
    for q, col in enumerate(cols):
        out = jnp.where(lane == q, col, out)
    return out


def contact_kernel(partner_s, arm_ref, world_ref, next_ref, out_ref, done_ref, cand, gat, feat, right, lead, acc):
    clumps = arm_ref.shape[1]
    done_ref[...] = jnp.zeros_like(done_ref)
    cand[:, 0:clumps, :] = world_ref[...]
    cand[:, clumps : 2 * clumps, :] = next_ref[...]
    zero = jnp.zeros((8, W), F32)
    for t in range(UNROLL):
        zero_tail(feat, t * FEATS * 8)
        zero_tail(right, t * FEATS * 8)
        for q in (4, 5, 6, 7, 12, 13, 14, 15):
            lead[t * W + 8 * q : t * W + 8 * q + 8, :] = zero
    upper = lax.broadcasted_iota(jnp.int32, (16, W), 0) < 8

    def group(i, carry):
        zas, ats = [], []
        for t in range(UNROLL):
            at = pl.multiple_of((i * UNROLL + t) * 8, 8)
            ats.append(at)
            for j in range(8):
                p = partner_s[0, at + j]
                for q in range(3):
                    spot = 24 * t + 8 * q + j
                    gat[spot : spot + 1, :] = cand[q, pl.ds(p, 1), :]
            za = [world_ref[q, pl.ds(at, 8), :] - 0.5 for q in range(3)]
            zas.append(za)
            scaled = [split3(v * (2.0 * C_CONTACT)) for v in za]
            put_rows(right, right_rows(*scaled, norm_of(*za, C_CONTACT)), t * FEATS * 8)
        for t in range(UNROLL):
            zb = [gat[24 * t + 8 * q : 24 * t + 8 * q + 8, :] - 0.5 for q in range(3)]
            parts = [split3(v) for v in zb]
            put_rows(feat, left_rows(*parts, norm_of(*zb, C_CONTACT)), t * FEATS * 8)
            for q, v in enumerate(zb + [jnp.ones((8, W), F32)]):
                hi = v.astype(BF).astype(F32)
                spot = t * W + 8 * q
                lead[spot : spot + 8, :] = hi
                lead[spot + 64 : spot + 72, :] = v - hi
        for t in range(UNROLL):
            for j in range(8):
                lhs = jnp.transpose(take_rows(feat, j, t * FEATS * 8)).astype(BF)
                kernel = gauss(lhs, take_rows(right, j, t * FEATS * 8).astype(BF))
                l16 = lead[pl.ds(t * W + j, 16, stride=8), :]
                both = jnp.concatenate([l16, jnp.where(upper, l16, 0.0)], axis=1).astype(BF)
                res = jnp.dot(both, two_halves(kernel), preferred_element_type=F32)
                spot = 64 * t + 8 * j
                acc[spot : spot + 8, :] = res[0:8] + res[8:16]
        for t in range(UNROLL):
            at, za = ats[t], zas[t]
            s = [acc[pl.ds(64 * t + q, 8, stride=8), :] for q in range(4)]
            f = [STIFF * (za[q] * s[3] - s[q]) for q in range(3)]
            arm = [arm_ref[q, pl.ds(at, 8), :] for q in range(3)]
            tq = [arm[1] * f[2] - arm[2] * f[1], arm[2] * f[0] - arm[0] * f[2],
                  arm[0] * f[1] - arm[1] * f[0]]
            out_ref[pl.ds(at, 8), :] = columns_to_lanes([lane_sum(v) for v in f + tq])
        return carry

    lax.fori_loop(0, clumps // (8 * UNROLL), group, 0)


def contact(partner, arms, world, following):
    clumps = arms.shape[1]
    vm = pl.BlockSpec(memory_space=pltpu.VMEM)
    sm = pl.BlockSpec(memory_space=pltpu.SMEM)
    return pl.pallas_call(
        contact_kernel,
        out_shape=(jax.ShapeDtypeStruct((clumps, W), F32), jax.ShapeDtypeStruct((8, W), F32)),
        in_specs=[sm, vm, vm, vm],
        out_specs=(vm, vm),
        scratch_shapes=[
            pltpu.VMEM((3, 2 * clumps, W), F32),
            pltpu.VMEM((UNROLL * 24, W), F32),
            pltpu.VMEM((UNROLL * FEATS * 8, W), F32),
            pltpu.VMEM((UNROLL * FEATS * 8, W), F32),
            pltpu.VMEM((UNROLL * W, W), F32),
            pltpu.VMEM((UNROLL * 64, W), F32),
        ],
        compiler_params=pltpu.CompilerParams(vmem_limit_bytes=10 << 20),
        name="contact",
    )(partner, arms, world, following)


def fluid_kernel(y_ref, table_ref, amp_ref, out_ref, names, names_s, right, acc, sems):
    for t in range(GROUPS):
        zero_tail(right, t * FEATS * 8)
    lane = lax.broadcasted_iota(jnp.int32, (8, W), 1)
    mine = (lane >> 4) == lax.broadcasted_iota(jnp.int32, (8, W), 0)
    place = lane & 15
    devices = out_ref.shape[0] // 2

    def read(g, carry):
        names[pl.ds(g, 1), :] = y_ref[pl.ds(g * ROWS + 48, 1), :].astype(jnp.int32) - 1
        return carry

    lax.fori_loop(0, devices, read, 0, unroll=8)
    move = pltpu.make_async_copy(names, names_s, sems.at[0])
    move.start()
    move.wait()

    def group(i, carry):
        ys, valids = [], []
        for t in range(GROUPS):
            g = i * (GROUPS // 2) + t // 2
            at = g * ROWS + (t % 2) * 8
            y = [y_ref[pl.ds(at + 16 * q, 8), :] for q in range(3)]
            ys.append(y)
            u = [v - 0.5 for v in y]
            scaled = [split3(v * (2.0 * C_FLUID)) for v in u]
            put_rows(right, right_rows(*scaled, norm_of(*u, C_FLUID)), t * FEATS * 8)
        for t in range(GROUPS):
            g = i * (GROUPS // 2) + t // 2
            valid = jnp.zeros((1, W), jnp.int32)
            for j in range(8):
                name = names_s[g, (t % 2) * 8 + j]
                valid = jnp.where((lane[0:1] >> 4) == j, name, valid)
                b = jnp.maximum(name, 0)
                kernel = gauss(table_ref[b], take_rows(right, j, t * FEATS * 8).astype(BF))
                res = jnp.dot(amp_ref[b], two_halves(kernel), preferred_element_type=F32)
                spot = 64 * t + 8 * j
                acc[spot : spot + 8, :] = res[0:8] + res[8:16]
            valids.append(valid)
        for t in range(GROUPS):
            g = i * (GROUPS // 2) + t // 2
            y = ys[t]
            s = [acc[pl.ds(64 * t + q, 8, stride=8), :] for q in range(4)]
            cross = [y[1] * s[2] - y[2] * s[1], y[2] * s[0] - y[0] * s[2],
                     y[0] * s[1] - y[1] * s[0]]
            moment = [y[q] * s[3] for q in range(3)]
            out = jnp.zeros((8, W), F32)
            for q, v in enumerate(s + cross + moment):
                out = jnp.where(place == q, lane_sum(v), out)
            row = jnp.sum(jnp.where(mine, out, 0.0), axis=0, keepdims=True)
            out_ref[pl.ds(2 * g + t % 2, 1), :] = jnp.where(valids[t] >= 0, row, 0.0)
        return carry

    lax.fori_loop(0, devices // (GROUPS // 2), group, 0)


def fluid(spots, table, amp):
    vm = pl.BlockSpec(memory_space=pltpu.VMEM)
    return pl.pallas_call(
        fluid_kernel,
        out_shape=jax.ShapeDtypeStruct((2 * W, W), F32),
        in_specs=[vm] * 3,
        out_specs=vm,
        scratch_shapes=[
            pltpu.VMEM((W, W), jnp.int32),
            pltpu.SMEM((W, W), jnp.int32),
            pltpu.VMEM((GROUPS * FEATS * 8, W), F32),
            pltpu.VMEM((GROUPS * 64, W), F32),
            pltpu.SemaphoreType.DMA((1,)),
        ],
        compiler_params=pltpu.CompilerParams(vmem_limit_bytes=14 << 20),
        name="fluid",
    )(spots, table, amp)


def combine_kernel(dev_ref, rank_ref, off_ref, vel_ref, got_ref, contact_ref, out_ref):
    entries = dev_ref.shape[1]
    clumps = entries // 2
    row = lax.broadcasted_iota(jnp.int32, (W, entries), 0)
    hot = (row == dev_ref[...]).astype(BF)
    rank = rank_ref[...]
    picked = jnp.zeros((16, entries), F32)
    for chunk in range(2):
        spread = jnp.zeros((W, entries), F32)
        for part in split3(jnp.transpose(got_ref[pl.ds(chunk, W, stride=2), :])):
            spread = spread + jnp.dot(part.astype(BF), hot, preferred_element_type=F32)
        spread = jnp.where((row >> 4) + 8 * chunk == rank, spread, 0.0)
        picked = picked + jnp.sum(spread.reshape(8, 16, entries), axis=0)
    touch = jnp.transpose(contact_ref[...])
    total = [touch[q : q + 1, :] for q in range(6)]
    v = [vel_ref[q : q + 1, :] for q in range(3)]
    for k in range(2):
        part = slice(k * clumps, k * clumps + clumps)
        g = [picked[q : q + 1, part] for q in range(10)]
        off = [off_ref[q : q + 1, part] for q in range(3)]
        f = [g[q] - v[q] * g[3] for q in range(3)]
        m = g[7:10]
        for q in range(3):
            a, b = (q + 1) % 3, (q + 2) % 3
            t = g[4 + q] - (m[a] * v[b] - m[b] * v[a]) - (off[a] * f[b] - off[b] * f[a])
            total[q] = total[q] + DRAG * f[q]
            total[3 + q] = total[3 + q] + DRAG * t
    for q in range(6):
        out_ref[q : q + 1, :] = total[q]


def combine(dev, rank, off, vel, got, touch):
    vm = pl.BlockSpec(memory_space=pltpu.VMEM)
    return pl.pallas_call(
        combine_kernel,
        out_shape=jax.ShapeDtypeStruct((6, vel.shape[1]), F32),
        in_specs=[vm] * 6,
        out_specs=vm,
        compiler_params=pltpu.CompilerParams(vmem_limit_bytes=14 << 20),
        name="combine",
    )(dev, rank, off, vel, got, touch)


def extended(cells, sides):
    for axis, dim in sides:
        count = lax.axis_size(axis)
        ends = count - 1
        head = lax.slice_in_dim(cells, 0, 1, axis=dim)
        tail = lax.slice_in_dim(cells, cells.shape[dim] - 1, cells.shape[dim], axis=dim)
        cells = jnp.concatenate(
            [
                lax.ppermute(tail, axis, [(i, (i + 1) % count) for i in range(ends)]),
                cells,
                lax.ppermute(head, axis, [((i + 1) % count, i) for i in range(ends)]),
            ],
            axis=dim,
        )
    return cells


def gate_kernel(array_ref, after_ref, out_ref):
    del array_ref, after_ref, out_ref


def gated(array, after):
    hbm = pl.BlockSpec(memory_space=pltpu.HBM)
    return pl.pallas_call(
        gate_kernel,
        out_shape=jax.ShapeDtypeStruct(array.shape, array.dtype),
        in_specs=[hbm, pl.BlockSpec(memory_space=pl.ANY)],
        out_specs=hbm,
        input_output_aliases={0: 0},
        name="gate",
    )(array, after)


def swap_all(array):
    return lax.all_to_all(array, AXES, split_axis=0, concat_axis=0, tiled=True)


def body(
    fluid_pos,
    fluid_vel,
    fluid_mass,
    fluid_count,
    clump_center,
    clump_vel,
    clump_arm,
    margin_device,
    margin_block,
    margin_offset,
    contact_partner,
):
    rows_x, rows_y, width = fluid_mass.shape
    blocks = rows_x * rows_y
    clumps = clump_arm.shape[0]
    entries = 2 * clumps
    devices = lax.axis_size(AXES)
    arms = jnp.transpose(clump_arm, (1, 0, 2))
    dev = margin_device.T.reshape(1, entries)
    blk = margin_block.T.reshape(1, entries)
    off = jnp.transpose(margin_offset, (2, 1, 0)).reshape(3, entries)
    vel = clump_vel.T
    send, rank = prep(dev, blk, off, arms)
    ready = rank[0, 0] >= 0
    world = jnp.where(ready, arms + clump_center.T[:, :, None], 0.0)
    following = lax.ppermute(world, AXES, [(i, (i + devices - 1) % devices) for i in range(devices)])
    lanes = jnp.arange(width, dtype=jnp.int32)
    live = jnp.where(lanes[None, None, :] < fluid_count[..., None], fluid_mass, 0.0)
    planes = jnp.concatenate([jnp.moveaxis(fluid_pos, 2, 0), live[None]], axis=0)
    planes = jnp.where(ready, planes, 0.0)
    ext = extended(planes, (("stream", 1), ("span", 2)))
    ext = ext.reshape(4, (rows_x + 2) * (rows_y + 2), width)
    send = gated(send, ext[0, 0:8] + following[0, 0:8])
    got = swap_all(send.reshape(devices, 1, ROWS * width))
    touch, done = contact(contact_partner.reshape(1, clumps), arms, world, following)
    ext = jnp.pad(ext, ((0, 0), (0, 4), (0, 0)))
    own = planes.reshape(4, blocks, width)
    speed = jnp.moveaxis(fluid_vel, 2, 0).reshape(3, blocks, width)
    dens, table, amp = density(ext, own, fluid_mass.reshape(blocks, width), speed, done)
    sums = fluid(got.reshape(devices * ROWS, width), table, amp)
    back = swap_all(sums.reshape(devices, 1, 2 * width)).reshape(2 * devices, width)
    loads = combine(dev, rank, off, vel, back, touch)
    return (dens.reshape(rows_x, rows_y, width), loads)


def solution(mesh):
    in_specs = (
        P("stream", "span", None, None),
        P("stream", "span", None, None),
        P("stream", "span", None),
        P("stream", "span"),
        P(("stream", "span"), None),
        P(("stream", "span"), None),
        P(("stream", "span"), None, None),
        P(("stream", "span"), None),
        P(("stream", "span"), None),
        P(("stream", "span"), None, None),
        P(("stream", "span")),
    )
    out_specs = (P("stream", "span", None), P(None, ("stream", "span")))
    return jax.shard_map(body, mesh=mesh, in_specs=in_specs, out_specs=out_specs, check_vma=False)
```

```python
import functools
import math

import jax
import jax.numpy as jnp
from jax import lax
from jax.experimental import pallas as pl
from jax.experimental.pallas import tpu as pltpu
from jax.sharding import PartitionSpec as P

H_SQ = 0.25
SIG_SQ = 0.5
DENS = 0.03125
DRAG = 0.002
STIFF = 0.005
LOG2E = math.log2(math.e)
C_FLUID = LOG2E / H_SQ
C_CONTACT = LOG2E / SIG_SQ
AXES = ("stream", "span")
W = 128
FEATS = 32
ROWS = 49
UNROLL = 4
GROUPS = 32
DEAD = -30000.0
BF = jnp.bfloat16
F32 = jnp.float32


def split3(v):
    hi = v.astype(BF).astype(F32)
    rest = v - hi
    mid = rest.astype(BF).astype(F32)
    return hi, mid, rest - mid


def norm_of(x, y, z, coef):
    return (x * x + y * y + z * z) * (-coef)


def left_rows(xs, ys, zs, norm):
    h, m, low = ([c[i] for c in (xs, ys, zs)] for i in range(3))
    one = jnp.ones_like(h[0])
    return h + h + h + m + m + low + list(split3(norm)) + [one, one, one]


def right_rows(xs, ys, zs, norm):
    h, m, low = ([c[i] for c in (xs, ys, zs)] for i in range(3))
    one = jnp.ones_like(h[0])
    return h + m + low + h + m + h + [one, one, one] + list(split3(norm))


def put_rows(ref, rows, base=0):
    for i, row in enumerate(rows):
        ref[base + 8 * i : base + 8 * i + 8, :] = row


def zero_tail(ref, base=0):
    zero = jnp.zeros((8, W), F32)
    for i in range(24, FEATS):
        ref[base + 8 * i : base + 8 * i + 8, :] = zero


def take_rows(ref, j, base=0):
    return ref[pl.ds(base + j, FEATS, stride=8), :]


def gauss(left, right):
    return jnp.exp2(jnp.dot(left, right, preferred_element_type=F32))


def two_halves(kernel):
    hi = kernel.astype(BF)
    lo = (kernel - hi.astype(F32)).astype(BF)
    return jnp.concatenate([hi, lo], axis=0)


def lane_sum(v):
    return jnp.sum(v, axis=1, keepdims=True)


def prep_kernel(dev_ref, blk_ref, dev_s, off_s, arm_ref, send_ref, rank_ref, buf, rank_s, sems):
    entries = dev_ref.shape[1]
    parts = entries // W
    dev = dev_ref[...]
    row = lax.broadcasted_iota(jnp.int32, (W, entries), 0)
    hot = (row == dev).astype(F32)
    hot_b = hot.astype(BF)
    up = lax.broadcasted_iota(jnp.int32, (W, 2 * W), 0)
    lane = lax.broadcasted_iota(jnp.int32, (W, 2 * W), 1)
    tri = jnp.where(lane >= W, 1.0, jnp.where(up < lane, 1.0, 0.0)).astype(BF)
    carry = jnp.zeros((W, W), F32)
    ranks = []
    for part in range(parts):
        piece = slice(part * W, part * W + W)
        both = jnp.dot(hot_b[:, piece], tri, preferred_element_type=F32)
        ranks.append(jnp.sum(hot[:, piece] * (both[:, :W] + carry), axis=0, keepdims=True))
        carry = carry + both[:, W:]
    rank = jnp.concatenate(ranks, axis=1).astype(jnp.int32)
    rank_ref[...] = rank
    move = pltpu.make_async_copy(rank_ref, rank_s, sems.at[0])
    move.start()
    named = jnp.where(row == rank, blk_ref[...] + 1, 0).astype(F32).astype(BF)
    ids = lax.dot_general(hot_b, named, (((1,), (1,)), ((), ())), preferred_element_type=F32)
    for d in range(W):
        buf[d * ROWS + 48 : d * ROWS + 49, :] = ids[d : d + 1, :]
    move.wait()

    clumps = entries // 2

    def step(i, carry):
        for k in range(2):
            for j in range(8):
                c = i * 8 + j
                e = k * clumps + c
                base = dev_s[0, e] * ROWS + rank_s[0, e]
                for q in range(3):
                    buf[pl.ds(base + 16 * q, 1), :] = (
                        arm_ref[q, pl.ds(c, 1), :] + off_s[q, e]
                    )
        return carry

    lax.fori_loop(0, clumps // 8, step, 0)
    out = pltpu.make_async_copy(buf, send_ref, sems.at[0])
    out.start()
    out.wait()


def prep(dev, blk, off, arms):
    entries = dev.shape[1]
    vm = pl.BlockSpec(memory_space=pltpu.VMEM)
    sm = pl.BlockSpec(memory_space=pltpu.SMEM)
    hbm = pl.BlockSpec(memory_space=pltpu.HBM)
    return pl.pallas_call(
        prep_kernel,
        out_shape=(
            jax.ShapeDtypeStruct((W * ROWS, W), F32),
            jax.ShapeDtypeStruct((1, entries), jnp.int32),
        ),
        in_specs=[vm, vm, sm, sm, vm],
        out_specs=(hbm, vm),
        scratch_shapes=[
            pltpu.VMEM((W * ROWS, W), F32),
            pltpu.SMEM((1, entries), jnp.int32),
            pltpu.SemaphoreType.DMA((1,)),
        ],
        compiler_params=pltpu.CompilerParams(vmem_limit_bytes=40 << 20),
        name="prep",
    )(dev, blk, dev, off, arms)


def density_kernel(ext_ref, own_ref, mass_ref, vel_ref, dens_ref, table_ref, amp_ref,
                   feat, right, sums, left, wide):
    rows_y = 8
    zero_tail(feat)
    for s in range(9):
        zero_tail(right, s * FEATS * 8)

    def coords(ref, at):
        return [ref[q, pl.ds(at, 8), :] - 0.5 for q in range(3)]

    def ext_group(g, carry):
        at = pl.multiple_of(g * 8, 8)
        x, y, z = coords(ext_ref, at)
        m = ext_ref[3, pl.ds(at, 8), :]
        logm = jnp.where(m > 0.0, jnp.log2(jnp.where(m > 0.0, m, 1.0)), DEAD)
        norm = norm_of(x, y, z, C_FLUID) + logm
        put_rows(feat, left_rows(split3(x), split3(y), split3(z), norm))
        for j in range(8):
            left[at + j] = jnp.transpose(take_rows(feat, j)).astype(BF)
        return carry

    lax.fori_loop(0, ext_ref.shape[1] // 8, ext_group, 0)

    def own_row(a, carry):
        at = pl.multiple_of(a * 8, 8)
        x, y, z = coords(own_ref, at)
        xs = [x + 1.0, x, x - 1.0]
        ys = [y + 1.0, y, y - 1.0]
        scale = 2.0 * C_FLUID
        xsplit = [split3(v * scale) for v in xs]
        ysplit = [split3(v * scale) for v in ys]
        zsplit = split3(z * scale)
        for ix in range(3):
            for iy in range(3):
                norm = norm_of(xs[ix], ys[iy], z, C_FLUID)
                put_rows(right, right_rows(xsplit[ix], ysplit[iy], zsplit, norm),
                         (ix * 3 + iy) * FEATS * 8)

        def block(b, inner):
            total = jnp.zeros((8, W), F32)
            for ix in range(3):
                for iy in range(3):
                    rhs = take_rows(right, b, (ix * 3 + iy) * FEATS * 8).astype(BF)
                    lhs = left[(a + ix) * 10 + b + iy]
                    total = total + jnp.sum(gauss(lhs, rhs).reshape(16, 8, W), axis=0)
            sums[pl.ds(b, 1), :] = jnp.sum(total, axis=0, keepdims=True)
            return inner

        lax.fori_loop(0, rows_y, block, 0, unroll=4)
        density = DENS * (mass_ref[pl.ds(at, 8), :] + sums[...])
        dens_ref[pl.ds(at, 8), :] = density
        weight = own_ref[3, pl.ds(at, 8), :] / density
        parts = [vel_ref[q, pl.ds(at, 8), :] * weight for q in range(3)] + [weight]
        zero = jnp.zeros((8, W), F32)
        for q, v in enumerate(parts):
            hi = v.astype(BF).astype(F32)
            wide[8 * q : 8 * q + 8, :] = hi
            wide[8 * (q + 8) : 8 * (q + 8) + 8, :] = v - hi
        for q in (4, 5, 6, 7, 12, 13, 14, 15):
            wide[8 * q : 8 * q + 8, :] = zero
        norm = norm_of(x, y, z, C_FLUID)
        put_rows(feat, left_rows(split3(x), split3(y), split3(z), norm))
        upper = lax.broadcasted_iota(jnp.int32, (16, W), 0) < 8
        for j in range(8):
            table_ref[at + j] = jnp.transpose(take_rows(feat, j)).astype(BF)
            a16 = wide[pl.ds(j, 16, stride=8), :]
            amp_ref[at + j, :, 0:W] = a16.astype(BF)
            amp_ref[at + j, :, W : 2 * W] = jnp.where(upper, a16, 0.0).astype(BF)
        return carry

    lax.fori_loop(0, 8, own_row, 0)


def density(ext, own, mass, vel):
    blocks = mass.shape[0]
    vm = pl.BlockSpec(memory_space=pltpu.VMEM)
    return pl.pallas_call(
        density_kernel,
        out_shape=(
            jax.ShapeDtypeStruct((blocks, W), F32),
            jax.ShapeDtypeStruct((blocks, W, FEATS), BF),
            jax.ShapeDtypeStruct((blocks, 16, 2 * W), BF),
        ),
        in_specs=[vm] * 4,
        out_specs=(vm, vm, vm),
        scratch_shapes=[
            pltpu.VMEM((FEATS * 8, W), F32),
            pltpu.VMEM((9 * FEATS * 8, W), F32),
            pltpu.VMEM((8, W), F32),
            pltpu.VMEM((ext.shape[1], W, FEATS), BF),
            pltpu.VMEM((W, W), F32),
        ],
        compiler_params=pltpu.CompilerParams(vmem_limit_bytes=14 << 20),
        name="density",
    )(ext, own, mass, vel)


def columns_to_lanes(cols):
    lane = lax.broadcasted_iota(jnp.int32, (8, W), 1)
    out = jnp.zeros((8, W), F32)
    for q, col in enumerate(cols):
        out = jnp.where(lane == q, col, out)
    return out


def contact_kernel(partner_s, arm_ref, world_ref, next_ref, out_ref, done_ref, cand, gat, feat, right, lead, acc):
    clumps = arm_ref.shape[1]
    done_ref[...] = jnp.zeros_like(done_ref)
    cand[:, 0:clumps, :] = world_ref[...]
    cand[:, clumps : 2 * clumps, :] = next_ref[...]
    zero = jnp.zeros((8, W), F32)
    for t in range(UNROLL):
        zero_tail(feat, t * FEATS * 8)
        zero_tail(right, t * FEATS * 8)
        for q in (4, 5, 6, 7, 12, 13, 14, 15):
            lead[t * W + 8 * q : t * W + 8 * q + 8, :] = zero
    upper = lax.broadcasted_iota(jnp.int32, (16, W), 0) < 8

    def group(i, carry):
        zas, ats = [], []
        for t in range(UNROLL):
            at = pl.multiple_of((i * UNROLL + t) * 8, 8)
            ats.append(at)
            for j in range(8):
                p = partner_s[0, at + j]
                for q in range(3):
                    spot = 24 * t + 8 * q + j
                    gat[spot : spot + 1, :] = cand[q, pl.ds(p, 1), :]
            za = [world_ref[q, pl.ds(at, 8), :] - 0.5 for q in range(3)]
            zas.append(za)
            scaled = [split3(v * (2.0 * C_CONTACT)) for v in za]
            put_rows(right, right_rows(*scaled, norm_of(*za, C_CONTACT)), t * FEATS * 8)
        for t in range(UNROLL):
            zb = [gat[24 * t + 8 * q : 24 * t + 8 * q + 8, :] - 0.5 for q in range(3)]
            parts = [split3(v) for v in zb]
            put_rows(feat, left_rows(*parts, norm_of(*zb, C_CONTACT)), t * FEATS * 8)
            for q, v in enumerate(zb + [jnp.ones((8, W), F32)]):
                hi = v.astype(BF).astype(F32)
                spot = t * W + 8 * q
                lead[spot : spot + 8, :] = hi
                lead[spot + 64 : spot + 72, :] = v - hi
        for t in range(UNROLL):
            for j in range(8):
                lhs = jnp.transpose(take_rows(feat, j, t * FEATS * 8)).astype(BF)
                kernel = gauss(lhs, take_rows(right, j, t * FEATS * 8).astype(BF))
                l16 = lead[pl.ds(t * W + j, 16, stride=8), :]
                both = jnp.concatenate([l16, jnp.where(upper, l16, 0.0)], axis=1).astype(BF)
                res = jnp.dot(both, two_halves(kernel), preferred_element_type=F32)
                spot = 64 * t + 8 * j
                acc[spot : spot + 8, :] = res[0:8] + res[8:16]
        for t in range(UNROLL):
            at, za = ats[t], zas[t]
            s = [acc[pl.ds(64 * t + q, 8, stride=8), :] for q in range(4)]
            f = [STIFF * (za[q] * s[3] - s[q]) for q in range(3)]
            arm = [arm_ref[q, pl.ds(at, 8), :] for q in range(3)]
            tq = [arm[1] * f[2] - arm[2] * f[1], arm[2] * f[0] - arm[0] * f[2],
                  arm[0] * f[1] - arm[1] * f[0]]
            out_ref[pl.ds(at, 8), :] = columns_to_lanes([lane_sum(v) for v in f + tq])
        return carry

    lax.fori_loop(0, clumps // (8 * UNROLL), group, 0)


def contact(partner, arms, world, following):
    clumps = arms.shape[1]
    vm = pl.BlockSpec(memory_space=pltpu.VMEM)
    sm = pl.BlockSpec(memory_space=pltpu.SMEM)
    return pl.pallas_call(
        contact_kernel,
        out_shape=(jax.ShapeDtypeStruct((clumps, W), F32), jax.ShapeDtypeStruct((8, W), F32)),
        in_specs=[sm, vm, vm, vm],
        out_specs=(vm, vm),
        scratch_shapes=[
            pltpu.VMEM((3, 2 * clumps, W), F32),
            pltpu.VMEM((UNROLL * 24, W), F32),
            pltpu.VMEM((UNROLL * FEATS * 8, W), F32),
            pltpu.VMEM((UNROLL * FEATS * 8, W), F32),
            pltpu.VMEM((UNROLL * W, W), F32),
            pltpu.VMEM((UNROLL * 64, W), F32),
        ],
        compiler_params=pltpu.CompilerParams(vmem_limit_bytes=10 << 20),
        name="contact",
    )(partner, arms, world, following)


def fluid_kernel(y_ref, table_ref, amp_ref, after_ref, out_ref, names, names_s, right, acc, sems):
    for t in range(GROUPS):
        zero_tail(right, t * FEATS * 8)
    lane = lax.broadcasted_iota(jnp.int32, (8, W), 1)
    mine = (lane >> 4) == lax.broadcasted_iota(jnp.int32, (8, W), 0)
    place = lane & 15
    devices = out_ref.shape[0] // 2

    def read(g, carry):
        names[pl.ds(g, 1), :] = y_ref[pl.ds(g * ROWS + 48, 1), :].astype(jnp.int32) - 1
        return carry

    lax.fori_loop(0, devices, read, 0, unroll=8)
    move = pltpu.make_async_copy(names, names_s, sems.at[0])
    move.start()
    move.wait()

    def group(i, carry):
        ys, valids = [], []
        for t in range(GROUPS):
            g = i * (GROUPS // 2) + t // 2
            at = g * ROWS + (t % 2) * 8
            y = [y_ref[pl.ds(at + 16 * q, 8), :] for q in range(3)]
            ys.append(y)
            u = [v - 0.5 for v in y]
            scaled = [split3(v * (2.0 * C_FLUID)) for v in u]
            put_rows(right, right_rows(*scaled, norm_of(*u, C_FLUID)), t * FEATS * 8)
        for t in range(GROUPS):
            g = i * (GROUPS // 2) + t // 2
            valid = jnp.zeros((1, W), jnp.int32)
            for j in range(8):
                name = names_s[g, (t % 2) * 8 + j]
                valid = jnp.where((lane[0:1] >> 4) == j, name, valid)
                b = jnp.maximum(name, 0)
                kernel = gauss(table_ref[b], take_rows(right, j, t * FEATS * 8).astype(BF))
                res = jnp.dot(amp_ref[b], two_halves(kernel), preferred_element_type=F32)
                spot = 64 * t + 8 * j
                acc[spot : spot + 8, :] = res[0:8] + res[8:16]
            valids.append(valid)
        for t in range(GROUPS):
            g = i * (GROUPS // 2) + t // 2
            y = ys[t]
            s = [acc[pl.ds(64 * t + q, 8, stride=8), :] for q in range(4)]
            cross = [y[1] * s[2] - y[2] * s[1], y[2] * s[0] - y[0] * s[2],
                     y[0] * s[1] - y[1] * s[0]]
            moment = [y[q] * s[3] for q in range(3)]
            out = jnp.zeros((8, W), F32)
            for q, v in enumerate(s + cross + moment):
                out = jnp.where(place == q, lane_sum(v), out)
            row = jnp.sum(jnp.where(mine, out, 0.0), axis=0, keepdims=True)
            out_ref[pl.ds(2 * g + t % 2, 1), :] = jnp.where(valids[t] >= 0, row, 0.0)
        return carry

    lax.fori_loop(0, devices // (GROUPS // 2), group, 0)


def fluid(spots, table, amp, after):
    vm = pl.BlockSpec(memory_space=pltpu.VMEM)
    return pl.pallas_call(
        fluid_kernel,
        out_shape=jax.ShapeDtypeStruct((2 * W, W), F32),
        in_specs=[vm] * 4,
        out_specs=vm,
        scratch_shapes=[
            pltpu.VMEM((W, W), jnp.int32),
            pltpu.SMEM((W, W), jnp.int32),
            pltpu.VMEM((GROUPS * FEATS * 8, W), F32),
            pltpu.VMEM((GROUPS * 64, W), F32),
            pltpu.SemaphoreType.DMA((1,)),
        ],
        compiler_params=pltpu.CompilerParams(vmem_limit_bytes=14 << 20),
        name="fluid",
    )(spots, table, amp, after)


def combine_kernel(dev_ref, rank_ref, off_ref, vel_ref, got_ref, contact_ref, out_ref):
    entries = dev_ref.shape[1]
    clumps = entries // 2
    row = lax.broadcasted_iota(jnp.int32, (W, entries), 0)
    hot = (row == dev_ref[...]).astype(BF)
    rank = rank_ref[...]
    picked = jnp.zeros((16, entries), F32)
    for chunk in range(2):
        spread = jnp.zeros((W, entries), F32)
        for part in split3(jnp.transpose(got_ref[pl.ds(chunk, W, stride=2), :])):
            spread = spread + jnp.dot(part.astype(BF), hot, preferred_element_type=F32)
        spread = jnp.where((row >> 4) + 8 * chunk == rank, spread, 0.0)
        picked = picked + jnp.sum(spread.reshape(8, 16, entries), axis=0)
    touch = jnp.transpose(contact_ref[...])
    total = [touch[q : q + 1, :] for q in range(6)]
    v = [vel_ref[q : q + 1, :] for q in range(3)]
    for k in range(2):
        part = slice(k * clumps, k * clumps + clumps)
        g = [picked[q : q + 1, part] for q in range(10)]
        off = [off_ref[q : q + 1, part] for q in range(3)]
        f = [g[q] - v[q] * g[3] for q in range(3)]
        m = g[7:10]
        for q in range(3):
            a, b = (q + 1) % 3, (q + 2) % 3
            t = g[4 + q] - (m[a] * v[b] - m[b] * v[a]) - (off[a] * f[b] - off[b] * f[a])
            total[q] = total[q] + DRAG * f[q]
            total[3 + q] = total[3 + q] + DRAG * t
    for q in range(6):
        out_ref[q : q + 1, :] = total[q]


def combine(dev, rank, off, vel, got, touch):
    vm = pl.BlockSpec(memory_space=pltpu.VMEM)
    return pl.pallas_call(
        combine_kernel,
        out_shape=jax.ShapeDtypeStruct((6, vel.shape[1]), F32),
        in_specs=[vm] * 6,
        out_specs=vm,
        compiler_params=pltpu.CompilerParams(vmem_limit_bytes=14 << 20),
        name="combine",
    )(dev, rank, off, vel, got, touch)


def extended(cells, sides):
    for axis, dim in sides:
        count = lax.axis_size(axis)
        ends = count - 1
        head = lax.slice_in_dim(cells, 0, 1, axis=dim)
        tail = lax.slice_in_dim(cells, cells.shape[dim] - 1, cells.shape[dim], axis=dim)
        cells = jnp.concatenate(
            [
                lax.ppermute(tail, axis, [(i, (i + 1) % count) for i in range(ends)]),
                cells,
                lax.ppermute(head, axis, [((i + 1) % count, i) for i in range(ends)]),
            ],
            axis=dim,
        )
    return cells


def gate_kernel(array_ref, after_ref, out_ref):
    del array_ref, after_ref, out_ref


def gated(array, after):
    hbm = pl.BlockSpec(memory_space=pltpu.HBM)
    return pl.pallas_call(
        gate_kernel,
        out_shape=jax.ShapeDtypeStruct(array.shape, array.dtype),
        in_specs=[hbm, pl.BlockSpec(memory_space=pl.ANY)],
        out_specs=hbm,
        input_output_aliases={0: 0},
        name="gate",
    )(array, after)


def swap_all(array):
    return lax.all_to_all(array, AXES, split_axis=0, concat_axis=0, tiled=True)


def body(
    fluid_pos,
    fluid_vel,
    fluid_mass,
    fluid_count,
    clump_center,
    clump_vel,
    clump_arm,
    margin_device,
    margin_block,
    margin_offset,
    contact_partner,
):
    rows_x, rows_y, width = fluid_mass.shape
    blocks = rows_x * rows_y
    clumps = clump_arm.shape[0]
    entries = 2 * clumps
    devices = lax.axis_size(AXES)
    arms = jnp.transpose(clump_arm, (1, 0, 2))
    dev = margin_device.T.reshape(1, entries)
    blk = margin_block.T.reshape(1, entries)
    off = jnp.transpose(margin_offset, (2, 1, 0)).reshape(3, entries)
    vel = clump_vel.T
    send, rank = prep(dev, blk, off, arms)
    ready = rank[0, 0] >= 0
    world = jnp.where(ready, arms + clump_center.T[:, :, None], 0.0)
    following = lax.ppermute(world, AXES, [(i, (i + devices - 1) % devices) for i in range(devices)])
    lanes = jnp.arange(width, dtype=jnp.int32)
    live = jnp.where(lanes[None, None, :] < fluid_count[..., None], fluid_mass, 0.0)
    planes = jnp.concatenate([jnp.moveaxis(fluid_pos, 2, 0), live[None]], axis=0)
    ext = extended(planes, (("stream", 1), ("span", 2)))
    ext = ext.reshape(4, (rows_x + 2) * (rows_y + 2), width)
    send = gated(send, ext[0, 0:8])
    got = swap_all(send.reshape(devices, 1, ROWS * width))
    ext = jnp.pad(ext, ((0, 0), (0, 4), (0, 0)))
    own = planes.reshape(4, blocks, width)
    speed = jnp.moveaxis(fluid_vel, 2, 0).reshape(3, blocks, width)
    dens, table, amp = density(ext, own, fluid_mass.reshape(blocks, width), speed)
    touch, done = contact(contact_partner.reshape(1, clumps), arms, world, following)
    sums = fluid(got.reshape(devices * ROWS, width), table, amp, done)
    back = swap_all(sums.reshape(devices, 1, 2 * width)).reshape(2 * devices, width)
    loads = combine(dev, rank, off, vel, back, touch)
    return (dens.reshape(rows_x, rows_y, width), loads)


def solution(mesh):
    in_specs = (
        P("stream", "span", None, None),
        P("stream", "span", None, None),
        P("stream", "span", None),
        P("stream", "span"),
        P(("stream", "span"), None),
        P(("stream", "span"), None),
        P(("stream", "span"), None, None),
        P(("stream", "span"), None),
        P(("stream", "span"), None),
        P(("stream", "span"), None, None),
        P(("stream", "span")),
    )
    out_specs = (P("stream", "span", None), P(None, ("stream", "span")))
    return jax.shard_map(body, mesh=mesh, in_specs=in_specs, out_specs=out_specs, check_vma=False)
```

```python
import functools
import math

import jax
import jax.numpy as jnp
from jax import lax
from jax.experimental import pallas as pl
from jax.experimental.pallas import tpu as pltpu
from jax.sharding import PartitionSpec as P

H_SQ = 0.25
SIG_SQ = 0.5
DENS = 0.03125
DRAG = 0.002
STIFF = 0.005
LOG2E = math.log2(math.e)
C_FLUID = LOG2E / H_SQ
C_CONTACT = LOG2E / SIG_SQ
AXES = ("stream", "span")
W = 128
FEATS = 32
ROWS = 49
UNROLL = 4
GROUPS = 32
DEAD = -30000.0
BF = jnp.bfloat16
F32 = jnp.float32


def split3(v):
    hi = v.astype(BF).astype(F32)
    rest = v - hi
    mid = rest.astype(BF).astype(F32)
    return hi, mid, rest - mid


def norm_of(x, y, z, coef):
    return (x * x + y * y + z * z) * (-coef)


def left_rows(xs, ys, zs, norm):
    h, m, low = ([c[i] for c in (xs, ys, zs)] for i in range(3))
    one = jnp.ones_like(h[0])
    return h + h + h + m + m + low + list(split3(norm)) + [one, one, one]


def right_rows(xs, ys, zs, norm):
    h, m, low = ([c[i] for c in (xs, ys, zs)] for i in range(3))
    one = jnp.ones_like(h[0])
    return h + m + low + h + m + h + [one, one, one] + list(split3(norm))


def put_rows(ref, rows, base=0):
    for i, row in enumerate(rows):
        ref[base + 8 * i : base + 8 * i + 8, :] = row


def zero_tail(ref, base=0):
    zero = jnp.zeros((8, W), F32)
    for i in range(24, FEATS):
        ref[base + 8 * i : base + 8 * i + 8, :] = zero


def take_rows(ref, j, base=0):
    return ref[pl.ds(base + j, FEATS, stride=8), :]


def gauss(left, right):
    return jnp.exp2(jnp.dot(left, right, preferred_element_type=F32))


def two_halves(kernel):
    hi = kernel.astype(BF)
    lo = (kernel - hi.astype(F32)).astype(BF)
    return jnp.concatenate([hi, lo], axis=0)


def lane_sum(v):
    return jnp.sum(v, axis=1, keepdims=True)


def prep_kernel(dev_ref, blk_ref, dev_s, off_s, arm_ref, send_ref, rank_ref, buf, rank_s, sems):
    entries = dev_ref.shape[1]
    parts = entries // W
    dev = dev_ref[...]
    row = lax.broadcasted_iota(jnp.int32, (W, entries), 0)
    hot = (row == dev).astype(F32)
    hot_b = hot.astype(BF)
    up = lax.broadcasted_iota(jnp.int32, (W, 2 * W), 0)
    lane = lax.broadcasted_iota(jnp.int32, (W, 2 * W), 1)
    tri = jnp.where(lane >= W, 1.0, jnp.where(up < lane, 1.0, 0.0)).astype(BF)
    carry = jnp.zeros((W, W), F32)
    ranks = []
    for part in range(parts):
        piece = slice(part * W, part * W + W)
        both = jnp.dot(hot_b[:, piece], tri, preferred_element_type=F32)
        ranks.append(jnp.sum(hot[:, piece] * (both[:, :W] + carry), axis=0, keepdims=True))
        carry = carry + both[:, W:]
    rank = jnp.concatenate(ranks, axis=1).astype(jnp.int32)
    rank_ref[...] = rank
    move = pltpu.make_async_copy(rank_ref, rank_s, sems.at[0])
    move.start()
    named = jnp.where(row == rank, blk_ref[...] + 1, 0).astype(F32).astype(BF)
    ids = lax.dot_general(hot_b, named, (((1,), (1,)), ((), ())), preferred_element_type=F32)
    for d in range(W):
        buf[d * ROWS + 48 : d * ROWS + 49, :] = ids[d : d + 1, :]
    move.wait()

    clumps = entries // 2

    def step(i, carry):
        for k in range(2):
            for j in range(8):
                c = i * 8 + j
                e = k * clumps + c
                base = dev_s[0, e] * ROWS + rank_s[0, e]
                for q in range(3):
                    buf[pl.ds(base + 16 * q, 1), :] = (
                        arm_ref[q, pl.ds(c, 1), :] + off_s[q, e]
                    )
        return carry

    lax.fori_loop(0, clumps // 8, step, 0)
    out = pltpu.make_async_copy(buf, send_ref, sems.at[0])
    out.start()
    out.wait()


def prep(dev, blk, off, arms):
    entries = dev.shape[1]
    vm = pl.BlockSpec(memory_space=pltpu.VMEM)
    sm = pl.BlockSpec(memory_space=pltpu.SMEM)
    hbm = pl.BlockSpec(memory_space=pltpu.HBM)
    return pl.pallas_call(
        prep_kernel,
        out_shape=(
            jax.ShapeDtypeStruct((W * ROWS, W), F32),
            jax.ShapeDtypeStruct((1, entries), jnp.int32),
        ),
        in_specs=[vm, vm, sm, sm, vm],
        out_specs=(hbm, vm),
        scratch_shapes=[
            pltpu.VMEM((W * ROWS, W), F32),
            pltpu.SMEM((1, entries), jnp.int32),
            pltpu.SemaphoreType.DMA((1,)),
        ],
        compiler_params=pltpu.CompilerParams(vmem_limit_bytes=40 << 20),
        name="prep",
    )(dev, blk, dev, off, arms)


def density_kernel(ext_ref, own_ref, mass_ref, vel_ref, dens_ref, table_ref, amp_ref,
                   feat, right, sums, left, wide):
    rows_y = 8
    zero_tail(feat)
    for s in range(9):
        zero_tail(right, s * FEATS * 8)

    def coords(ref, at):
        return [ref[q, pl.ds(at, 8), :] - 0.5 for q in range(3)]

    def ext_group(g, carry):
        at = pl.multiple_of(g * 8, 8)
        x, y, z = coords(ext_ref, at)
        m = ext_ref[3, pl.ds(at, 8), :]
        logm = jnp.where(m > 0.0, jnp.log2(jnp.where(m > 0.0, m, 1.0)), DEAD)
        norm = norm_of(x, y, z, C_FLUID) + logm
        put_rows(feat, left_rows(split3(x), split3(y), split3(z), norm))
        for j in range(8):
            left[at + j] = jnp.transpose(take_rows(feat, j)).astype(BF)
        return carry

    lax.fori_loop(0, ext_ref.shape[1] // 8, ext_group, 0)

    def own_row(a, carry):
        at = pl.multiple_of(a * 8, 8)
        x, y, z = coords(own_ref, at)
        xs = [x + 1.0, x, x - 1.0]
        ys = [y + 1.0, y, y - 1.0]
        scale = 2.0 * C_FLUID
        xsplit = [split3(v * scale) for v in xs]
        ysplit = [split3(v * scale) for v in ys]
        zsplit = split3(z * scale)
        for ix in range(3):
            for iy in range(3):
                norm = norm_of(xs[ix], ys[iy], z, C_FLUID)
                put_rows(right, right_rows(xsplit[ix], ysplit[iy], zsplit, norm),
                         (ix * 3 + iy) * FEATS * 8)

        def block(b, inner):
            total = jnp.zeros((8, W), F32)
            for ix in range(3):
                for iy in range(3):
                    rhs = take_rows(right, b, (ix * 3 + iy) * FEATS * 8).astype(BF)
                    lhs = left[(a + ix) * 10 + b + iy]
                    total = total + jnp.sum(gauss(lhs, rhs).reshape(16, 8, W), axis=0)
            sums[pl.ds(b, 1), :] = jnp.sum(total, axis=0, keepdims=True)
            return inner

        lax.fori_loop(0, rows_y, block, 0, unroll=4)
        density = DENS * (mass_ref[pl.ds(at, 8), :] + sums[...])
        dens_ref[pl.ds(at, 8), :] = density
        weight = own_ref[3, pl.ds(at, 8), :] / density
        parts = [vel_ref[q, pl.ds(at, 8), :] * weight for q in range(3)] + [weight]
        zero = jnp.zeros((8, W), F32)
        for q, v in enumerate(parts):
            hi = v.astype(BF).astype(F32)
            wide[8 * q : 8 * q + 8, :] = hi
            wide[8 * (q + 8) : 8 * (q + 8) + 8, :] = v - hi
        for q in (4, 5, 6, 7, 12, 13, 14, 15):
            wide[8 * q : 8 * q + 8, :] = zero
        norm = norm_of(x, y, z, C_FLUID)
        put_rows(feat, left_rows(split3(x), split3(y), split3(z), norm))
        upper = lax.broadcasted_iota(jnp.int32, (16, W), 0) < 8
        for j in range(8):
            table_ref[at + j] = jnp.transpose(take_rows(feat, j)).astype(BF)
            a16 = wide[pl.ds(j, 16, stride=8), :]
            amp_ref[at + j, :, 0:W] = a16.astype(BF)
            amp_ref[at + j, :, W : 2 * W] = jnp.where(upper, a16, 0.0).astype(BF)
        return carry

    lax.fori_loop(0, 8, own_row, 0)


def density(ext, own, mass, vel):
    blocks = mass.shape[0]
    vm = pl.BlockSpec(memory_space=pltpu.VMEM)
    return pl.pallas_call(
        density_kernel,
        out_shape=(
            jax.ShapeDtypeStruct((blocks, W), F32),
            jax.ShapeDtypeStruct((blocks, W, FEATS), BF),
            jax.ShapeDtypeStruct((blocks, 16, 2 * W), BF),
        ),
        in_specs=[vm] * 4,
        out_specs=(vm, vm, vm),
        scratch_shapes=[
            pltpu.VMEM((FEATS * 8, W), F32),
            pltpu.VMEM((9 * FEATS * 8, W), F32),
            pltpu.VMEM((8, W), F32),
            pltpu.VMEM((ext.shape[1], W, FEATS), BF),
            pltpu.VMEM((W, W), F32),
        ],
        compiler_params=pltpu.CompilerParams(vmem_limit_bytes=14 << 20),
        name="density",
    )(ext, own, mass, vel)


def columns_to_lanes(cols):
    lane = lax.broadcasted_iota(jnp.int32, (8, W), 1)
    out = jnp.zeros((8, W), F32)
    for q, col in enumerate(cols):
        out = jnp.where(lane == q, col, out)
    return out


def contact_kernel(partner_s, arm_ref, world_ref, next_ref, after_ref, out_ref, done_ref, cand, gat, feat, right, lead, acc):
    clumps = arm_ref.shape[1]
    done_ref[...] = jnp.zeros_like(done_ref)
    cand[:, 0:clumps, :] = world_ref[...]
    cand[:, clumps : 2 * clumps, :] = next_ref[...]
    zero = jnp.zeros((8, W), F32)
    for t in range(UNROLL):
        zero_tail(feat, t * FEATS * 8)
        zero_tail(right, t * FEATS * 8)
        for q in (4, 5, 6, 7, 12, 13, 14, 15):
            lead[t * W + 8 * q : t * W + 8 * q + 8, :] = zero
    upper = lax.broadcasted_iota(jnp.int32, (16, W), 0) < 8

    def group(i, carry):
        zas, ats = [], []
        for t in range(UNROLL):
            at = pl.multiple_of((i * UNROLL + t) * 8, 8)
            ats.append(at)
            for j in range(8):
                p = partner_s[0, at + j]
                for q in range(3):
                    spot = 24 * t + 8 * q + j
                    gat[spot : spot + 1, :] = cand[q, pl.ds(p, 1), :]
            za = [world_ref[q, pl.ds(at, 8), :] - 0.5 for q in range(3)]
            zas.append(za)
            scaled = [split3(v * (2.0 * C_CONTACT)) for v in za]
            put_rows(right, right_rows(*scaled, norm_of(*za, C_CONTACT)), t * FEATS * 8)
        for t in range(UNROLL):
            zb = [gat[24 * t + 8 * q : 24 * t + 8 * q + 8, :] - 0.5 for q in range(3)]
            parts = [split3(v) for v in zb]
            put_rows(feat, left_rows(*parts, norm_of(*zb, C_CONTACT)), t * FEATS * 8)
            for q, v in enumerate(zb + [jnp.ones((8, W), F32)]):
                hi = v.astype(BF).astype(F32)
                spot = t * W + 8 * q
                lead[spot : spot + 8, :] = hi
                lead[spot + 64 : spot + 72, :] = v - hi
        for t in range(UNROLL):
            for j in range(8):
                lhs = jnp.transpose(take_rows(feat, j, t * FEATS * 8)).astype(BF)
                kernel = gauss(lhs, take_rows(right, j, t * FEATS * 8).astype(BF))
                l16 = lead[pl.ds(t * W + j, 16, stride=8), :]
                both = jnp.concatenate([l16, jnp.where(upper, l16, 0.0)], axis=1).astype(BF)
                res = jnp.dot(both, two_halves(kernel), preferred_element_type=F32)
                spot = 64 * t + 8 * j
                acc[spot : spot + 8, :] = res[0:8] + res[8:16]
        for t in range(UNROLL):
            at, za = ats[t], zas[t]
            s = [acc[pl.ds(64 * t + q, 8, stride=8), :] for q in range(4)]
            f = [STIFF * (za[q] * s[3] - s[q]) for q in range(3)]
            arm = [arm_ref[q, pl.ds(at, 8), :] for q in range(3)]
            tq = [arm[1] * f[2] - arm[2] * f[1], arm[2] * f[0] - arm[0] * f[2],
                  arm[0] * f[1] - arm[1] * f[0]]
            out_ref[pl.ds(at, 8), :] = columns_to_lanes([lane_sum(v) for v in f + tq])
        return carry

    lax.fori_loop(0, clumps // (8 * UNROLL), group, 0)


def contact(partner, arms, world, following, after):
    clumps = arms.shape[1]
    vm = pl.BlockSpec(memory_space=pltpu.VMEM)
    sm = pl.BlockSpec(memory_space=pltpu.SMEM)
    return pl.pallas_call(
        contact_kernel,
        out_shape=(jax.ShapeDtypeStruct((clumps, W), F32), jax.ShapeDtypeStruct((8, W), F32)),
        in_specs=[sm, vm, vm, vm, pl.BlockSpec(memory_space=pl.ANY)],
        out_specs=(vm, vm),
        scratch_shapes=[
            pltpu.VMEM((3, 2 * clumps, W), F32),
            pltpu.VMEM((UNROLL * 24, W), F32),
            pltpu.VMEM((UNROLL * FEATS * 8, W), F32),
            pltpu.VMEM((UNROLL * FEATS * 8, W), F32),
            pltpu.VMEM((UNROLL * W, W), F32),
            pltpu.VMEM((UNROLL * 64, W), F32),
        ],
        compiler_params=pltpu.CompilerParams(vmem_limit_bytes=10 << 20),
        name="contact",
    )(partner, arms, world, following, after)


def fluid_kernel(y_ref, table_hbm, amp_hbm, after_ref, out_ref, names, names_s, right, acc,
                 table_ref, amp_ref, sems):
    load = [
        pltpu.make_async_copy(table_hbm, table_ref, sems.at[1]),
        pltpu.make_async_copy(amp_hbm, amp_ref, sems.at[2]),
    ]
    for copy in load:
        copy.start()
    for t in range(GROUPS):
        zero_tail(right, t * FEATS * 8)
    lane = lax.broadcasted_iota(jnp.int32, (8, W), 1)
    mine = (lane >> 4) == lax.broadcasted_iota(jnp.int32, (8, W), 0)
    place = lane & 15
    devices = out_ref.shape[0] // 2

    def read(g, carry):
        names[pl.ds(g, 1), :] = y_ref[pl.ds(g * ROWS + 48, 1), :].astype(jnp.int32) - 1
        return carry

    lax.fori_loop(0, devices, read, 0, unroll=8)
    move = pltpu.make_async_copy(names, names_s, sems.at[0])
    move.start()
    move.wait()
    for copy in load:
        copy.wait()

    def group(i, carry):
        ys, valids = [], []
        for t in range(GROUPS):
            g = i * (GROUPS // 2) + t // 2
            at = g * ROWS + (t % 2) * 8
            y = [y_ref[pl.ds(at + 16 * q, 8), :] for q in range(3)]
            ys.append(y)
            u = [v - 0.5 for v in y]
            scaled = [split3(v * (2.0 * C_FLUID)) for v in u]
            put_rows(right, right_rows(*scaled, norm_of(*u, C_FLUID)), t * FEATS * 8)
        for t in range(GROUPS):
            g = i * (GROUPS // 2) + t // 2
            valid = jnp.zeros((1, W), jnp.int32)
            for j in range(8):
                name = names_s[g, (t % 2) * 8 + j]
                valid = jnp.where((lane[0:1] >> 4) == j, name, valid)
                b = jnp.maximum(name, 0)
                kernel = gauss(table_ref[b], take_rows(right, j, t * FEATS * 8).astype(BF))
                res = jnp.dot(amp_ref[b], two_halves(kernel), preferred_element_type=F32)
                spot = 64 * t + 8 * j
                acc[spot : spot + 8, :] = res[0:8] + res[8:16]
            valids.append(valid)
        for t in range(GROUPS):
            g = i * (GROUPS // 2) + t // 2
            y = ys[t]
            s = [acc[pl.ds(64 * t + q, 8, stride=8), :] for q in range(4)]
            cross = [y[1] * s[2] - y[2] * s[1], y[2] * s[0] - y[0] * s[2],
                     y[0] * s[1] - y[1] * s[0]]
            moment = [y[q] * s[3] for q in range(3)]
            out = jnp.zeros((8, W), F32)
            for q, v in enumerate(s + cross + moment):
                out = jnp.where(place == q, lane_sum(v), out)
            row = jnp.sum(jnp.where(mine, out, 0.0), axis=0, keepdims=True)
            out_ref[pl.ds(2 * g + t % 2, 1), :] = jnp.where(valids[t] >= 0, row, 0.0)
        return carry

    lax.fori_loop(0, devices // (GROUPS // 2), group, 0)


def fluid(spots, table, amp, after):
    vm = pl.BlockSpec(memory_space=pltpu.VMEM)
    hbm = pl.BlockSpec(memory_space=pltpu.HBM)
    return pl.pallas_call(
        fluid_kernel,
        out_shape=jax.ShapeDtypeStruct((2 * W, W), F32),
        in_specs=[vm, hbm, hbm, hbm],
        out_specs=vm,
        scratch_shapes=[
            pltpu.VMEM((W, W), jnp.int32),
            pltpu.SMEM((W, W), jnp.int32),
            pltpu.VMEM((GROUPS * FEATS * 8, W), F32),
            pltpu.VMEM((GROUPS * 64, W), F32),
            pltpu.VMEM(table.shape, BF),
            pltpu.VMEM(amp.shape, BF),
            pltpu.SemaphoreType.DMA((3,)),
        ],
        compiler_params=pltpu.CompilerParams(vmem_limit_bytes=18 << 20),
        name="fluid",
    )(spots, table, amp, after)


def combine_kernel(dev_ref, rank_ref, off_ref, vel_ref, got_ref, contact_ref, out_ref):
    entries = dev_ref.shape[1]
    clumps = entries // 2
    row = lax.broadcasted_iota(jnp.int32, (W, entries), 0)
    hot = (row == dev_ref[...]).astype(BF)
    rank = rank_ref[...]
    picked = jnp.zeros((16, entries), F32)
    for chunk in range(2):
        spread = jnp.zeros((W, entries), F32)
        for part in split3(jnp.transpose(got_ref[pl.ds(chunk, W, stride=2), :])):
            spread = spread + jnp.dot(part.astype(BF), hot, preferred_element_type=F32)
        spread = jnp.where((row >> 4) + 8 * chunk == rank, spread, 0.0)
        picked = picked + jnp.sum(spread.reshape(8, 16, entries), axis=0)
    touch = jnp.transpose(contact_ref[...])
    total = [touch[q : q + 1, :] for q in range(6)]
    v = [vel_ref[q : q + 1, :] for q in range(3)]
    for k in range(2):
        part = slice(k * clumps, k * clumps + clumps)
        g = [picked[q : q + 1, part] for q in range(10)]
        off = [off_ref[q : q + 1, part] for q in range(3)]
        f = [g[q] - v[q] * g[3] for q in range(3)]
        m = g[7:10]
        for q in range(3):
            a, b = (q + 1) % 3, (q + 2) % 3
            t = g[4 + q] - (m[a] * v[b] - m[b] * v[a]) - (off[a] * f[b] - off[b] * f[a])
            total[q] = total[q] + DRAG * f[q]
            total[3 + q] = total[3 + q] + DRAG * t
    for q in range(6):
        out_ref[q : q + 1, :] = total[q]


def combine(dev, rank, off, vel, got, touch):
    vm = pl.BlockSpec(memory_space=pltpu.VMEM)
    return pl.pallas_call(
        combine_kernel,
        out_shape=jax.ShapeDtypeStruct((6, vel.shape[1]), F32),
        in_specs=[vm] * 6,
        out_specs=vm,
        compiler_params=pltpu.CompilerParams(vmem_limit_bytes=14 << 20),
        name="combine",
    )(dev, rank, off, vel, got, touch)


def extended(cells, sides):
    for axis, dim in sides:
        count = lax.axis_size(axis)
        ends = count - 1
        head = lax.slice_in_dim(cells, 0, 1, axis=dim)
        tail = lax.slice_in_dim(cells, cells.shape[dim] - 1, cells.shape[dim], axis=dim)
        cells = jnp.concatenate(
            [
                lax.ppermute(tail, axis, [(i, (i + 1) % count) for i in range(ends)]),
                cells,
                lax.ppermute(head, axis, [((i + 1) % count, i) for i in range(ends)]),
            ],
            axis=dim,
        )
    return cells


def swap_all(array):
    return lax.all_to_all(array, AXES, split_axis=0, concat_axis=0, tiled=True)


def body(
    fluid_pos,
    fluid_vel,
    fluid_mass,
    fluid_count,
    clump_center,
    clump_vel,
    clump_arm,
    margin_device,
    margin_block,
    margin_offset,
    contact_partner,
):
    rows_x, rows_y, width = fluid_mass.shape
    blocks = rows_x * rows_y
    clumps = clump_arm.shape[0]
    entries = 2 * clumps
    devices = lax.axis_size(AXES)
    arms = jnp.transpose(clump_arm, (1, 0, 2))
    world = arms + clump_center.T[:, :, None]
    following = lax.ppermute(world, AXES, [(i, (i + devices - 1) % devices) for i in range(devices)])
    lanes = jnp.arange(width, dtype=jnp.int32)
    live = jnp.where(lanes[None, None, :] < fluid_count[..., None], fluid_mass, 0.0)
    planes = jnp.concatenate([jnp.moveaxis(fluid_pos, 2, 0), live[None]], axis=0)
    tall = extended(planes, (("stream", 1),))
    dev = margin_device.T.reshape(1, entries)
    blk = margin_block.T.reshape(1, entries)
    off = jnp.transpose(margin_offset, (2, 1, 0)).reshape(3, entries)
    vel = clump_vel.T
    dev, tall = lax.optimization_barrier((dev, tall))
    ext = extended(tall, (("span", 2),))
    send, rank = prep(dev, blk, off, arms)
    send, ext, following = lax.optimization_barrier((send, ext, following))
    got = swap_all(send.reshape(devices, 1, ROWS * width))
    ext = ext.reshape(4, (rows_x + 2) * (rows_y + 2), width)
    ext = jnp.pad(ext, ((0, 0), (0, 4), (0, 0)))
    own = planes.reshape(4, blocks, width)
    speed = jnp.moveaxis(fluid_vel, 2, 0).reshape(3, blocks, width)
    dens, table, amp = density(ext, own, fluid_mass.reshape(blocks, width), speed)
    touch, done = contact(contact_partner.reshape(1, clumps), arms, world, following, dens)
    sums = fluid(got.reshape(devices * ROWS, width), table, amp, done)
    back = swap_all(sums.reshape(devices, 1, 2 * width)).reshape(2 * devices, width)
    loads = combine(dev, rank, off, vel, back, touch)
    return (dens.reshape(rows_x, rows_y, width), loads)


def solution(mesh):
    in_specs = (
        P("stream", "span", None, None),
        P("stream", "span", None, None),
        P("stream", "span", None),
        P("stream", "span"),
        P(("stream", "span"), None),
        P(("stream", "span"), None),
        P(("stream", "span"), None, None),
        P(("stream", "span"), None),
        P(("stream", "span"), None),
        P(("stream", "span"), None, None),
        P(("stream", "span")),
    )
    out_specs = (P("stream", "span", None), P(None, ("stream", "span")))
    return jax.shard_map(body, mesh=mesh, in_specs=in_specs, out_specs=out_specs, check_vma=False)
```
